32 devices in a mesh: segment: 4 (over y, core), vol: 8 (over z, x).
Axes of the slice: x: 2, y: 2, z: 4, core: 2. Of those that a mesh axis runs over, the one named last changes fastest.
Arguments:
- cotangent: bfloat16 [64, 32, 256], P(None, 'vol'), may hold values from -6 to 6
- labels: int32 [32, 256], P('vol'), may hold values from 0 to 2
- class_weight: float32 [3], replicated, may hold values from 0.25 to 2
- inputs: bfloat16 [4, 64, 32, 256], P('segment', None, 'vol'), may hold values from -6 to 6
- fine_pre: bfloat16 [4, 64, 32, 256], P('segment', None, 'vol'), may hold values from -6 to 6
- pooled: bfloat16 [4, 64, 8, 128], P('segment', None, 'vol'), may hold values from -6 to 6
- coarse_pre: bfloat16 [4, 64, 8, 128], P('segment', None, 'vol'), may hold values from -6 to 6
- fine_filters: bfloat16 [4, 27, 64, 64], P('segment'), may hold values from -0.15625 to 0.15625
- coarse_filters: bfloat16 [4, 27, 64, 64], P('segment'), may hold values from -0.15625 to 0.15625
Outputs:
- input_grads: bfloat16 [4, 64, 32, 256], P('segment', None, 'vol')
- fine_filter_grads: float32 [4, 27, 64, 64], P('segment')
- coarse_filter_grads: float32 [4, 27, 64, 64], P('segment')
The draws below stay inside these ranges and needn't reach their ends.
Inputs may be any that keep to these rules, and one draw needn't show every extreme that they name: `labels`: 0 is background, 1 fault, 2 horizon.
All inputs are finite; a program needn't handle non-finite values.
Results may differ from the reference program's by a relative error of at most 0.02.
Values may be sent and summed in bfloat16 or wider, within the bound.
A program may use at most 64 MiB of HBM per device.

```python
import math
import jax
import jax.numpy as jnp
from jax import lax

C = 64
TAPS = 27
CLASSES = 3
XL = 16
SEGMENTS = 4
NDEP = 32
NI = 16
PLANE = 256
CROWS = 8
CPLANE = 128


def plant(entries, stream_key, least, largest):
    shape = entries.shape
    spot = [jax.random.randint(jax.random.fold_in(stream_key, axis), (), 0, shape[axis]) for axis in range(len(shape))]
    entries = entries.at[tuple(spot)].set(least)
    longest = shape.index(max(shape))
    spot[longest] = (spot[longest] + 1) % shape[longest]
    return entries.at[tuple(spot)].set(largest)


def steps_of(own_key, dims, cuts, least, top_value):
    factor_of, own = 1.0, jax.random.fold_in(own_key, 6)
    for axis_at, parts in cuts:
        draws = jnp.exp(jax.random.uniform(jax.random.fold_in(own, axis_at), (parts,), jnp.float32, least / len(cuts), top_value / len(cuts)))
        factor_of = factor_of * jnp.repeat(draws, dims[axis_at] // parts).reshape([-1 if axis == axis_at else 1 for axis in range(len(dims))])
    return factor_of


def noise(rng, dims, deviation, limit, cuts=(), kind=jnp.bfloat16):
    values = deviation * jax.random.normal(rng, dims, jnp.float32)
    if cuts:
        values = values * steps_of(rng, dims, cuts, -0.22, 0.18)
    return jnp.clip(values, -limit, limit).astype(kind)


def setup_inputs(seed: int = 0) -> dict:
    seeds = jax.random.split(jax.random.key(seed), 10)
    cotangent = noise(seeds[0], (C, NDEP, PLANE), 1.0, 6.0, ((1, 8),))
    labels = plant(jax.random.randint(seeds[1], (NDEP, PLANE), 0, 3), jax.random.fold_in(seeds[1], 1), 0, 2).astype(jnp.int32)
    class_weight = jnp.clip(jnp.exp(jax.random.uniform(seeds[2], (CLASSES,), jnp.float32, math.log(0.25), math.log(2.0))), 0.25, 2.0)
    inputs = noise(seeds[3], (SEGMENTS, C, NDEP, PLANE), 1.0, 6.0, ((0, 4), (2, 8)))
    fine_pre = noise(seeds[4], (SEGMENTS, C, NDEP, PLANE), 1.0, 6.0, ((0, 4), (2, 8)))
    pooled = noise(seeds[5], (SEGMENTS, C, CROWS, CPLANE), 1.0, 6.0, ((0, 4), (2, 8)))
    coarse_pre = noise(seeds[6], (SEGMENTS, C, CROWS, CPLANE), 1.0, 6.0, ((0, 4), (2, 8)))
    fine_filters = noise(seeds[7], (SEGMENTS, TAPS, C, C), (TAPS * C) ** -0.5, 0.15625, ((0, 4),))
    coarse_filters = noise(seeds[8], (SEGMENTS, TAPS, C, C), (TAPS * C) ** -0.5, 0.15625, ((0, 4),))
    return {"cotangent": cotangent, "labels": labels, "class_weight": class_weight, "inputs": inputs, "fine_pre": fine_pre, "pooled": pooled, "coarse_pre": coarse_pre, "fine_filters": fine_filters, "coarse_filters": coarse_filters}


def shift_volume(volume, depth_step, inline_step, cross_step):
    padded = jnp.pad(volume, ((0, 0), (1, 1), (1, 1), (1, 1)))
    depth_len, inline_len, cross_len = (volume.shape[1], volume.shape[2], volume.shape[3])
    return padded[:, 1 - depth_step:1 - depth_step + depth_len, 1 - inline_step:1 - inline_step + inline_len, 1 - cross_step:1 - cross_step + cross_len]

def conv_back(gradient, saved_input, weights):
    kernel = weights.astype(jnp.float32)
    grad_wide = gradient.astype(jnp.float32)
    saved_wide = saved_input.astype(jnp.float32)
    summed = jnp.zeros(grad_wide.shape, jnp.float32)
    filter_list = []
    for tap_index in range(27):
        shifted = shift_volume(grad_wide, tap_index // 9 - 1, tap_index // 3 % 3 - 1, tap_index % 3 - 1)
        summed = summed + jnp.einsum('io,oabc->iabc', kernel[tap_index], shifted, precision=lax.Precision.HIGHEST)
        filter_list.append(jnp.einsum('iabc,oabc->io', saved_wide, shifted, precision=lax.Precision.HIGHEST))
    return (summed, jnp.stack(filter_list))

def reference(cotangent, labels, class_weight, inputs, fine_pre, pooled, coarse_pre, fine_filters, coarse_filters):
    half_depth, half_inline, half_cross = (NDEP // 2, NI // 2, XL // 2)
    fine_scale = 1.0 / math.sqrt(NDEP * NI * XL)
    coarse_scale = 1.0 / math.sqrt(half_depth * half_inline * half_cross)
    cell_weight = class_weight[labels]
    gradient = (cotangent.astype(jnp.float32) * cell_weight[None]).astype(jnp.bfloat16).reshape(C, NDEP, NI, XL)
    grads_out = [None] * SEGMENTS
    fine_out = [None] * SEGMENTS
    coarse_out = [None] * SEGMENTS
    for segment_index in range(SEGMENTS - 1, -1, -1):
        saved_input = inputs[segment_index].reshape(C, NDEP, NI, XL)
        fine_gate = fine_pre[segment_index].reshape(C, NDEP, NI, XL)
        coarse_input = pooled[segment_index].reshape(C, half_inline, half_depth, half_cross).transpose(0, 2, 1, 3)
        coarse_gate = coarse_pre[segment_index].reshape(C, half_inline, half_depth, half_cross).transpose(0, 2, 1, 3)
        grad_wide = gradient.astype(jnp.float32)
        pooled_grad = grad_wide.reshape(C, half_depth, 2, half_inline, 2, half_cross, 2).sum(axis=(2, 4, 6)).astype(jnp.bfloat16)
        coarse_gz = jnp.where(coarse_gate > 0, pooled_grad, jnp.zeros_like(pooled_grad))
        coarse_back, coarse_filt = conv_back(coarse_gz, coarse_input, coarse_filters[segment_index])
        coarse_back = lax.optimization_barrier(coarse_back.astype(jnp.bfloat16)).astype(jnp.float32)
        spread = jnp.broadcast_to(coarse_back[:, :, None, :, None, :, None], (C, half_depth, 2, half_inline, 2, half_cross, 2)).reshape(C, NDEP, NI, XL)
        fine_grad = grad_wide + 0.125 * spread
        fine_gz = jnp.where(fine_gate > 0, fine_grad, jnp.zeros_like(fine_grad)).astype(jnp.bfloat16)
        fine_back, fine_filt = conv_back(fine_gz, saved_input, fine_filters[segment_index])
        gradient = (grad_wide + fine_back).astype(jnp.bfloat16)
        grads_out[segment_index] = gradient.reshape(C, NDEP, NI * XL)
        fine_out[segment_index] = fine_filt * fine_scale
        coarse_out[segment_index] = coarse_filt * coarse_scale
    return (jnp.stack(grads_out), jnp.stack(fine_out), jnp.stack(coarse_out))
```

```python
import functools
import math

import jax
import jax.numpy as jnp
from jax import lax
from jax.experimental import pallas as pl
from jax.experimental.pallas import tpu as pltpu
from jax.sharding import PartitionSpec as P

XL = 16
HX = XL // 2
TAPS = 27
BF = jnp.bfloat16
F32 = jnp.float32


def iota(shape, dim):
    return lax.broadcasted_iota(jnp.int32, shape, dim)


def matmul(a, b):
    return lax.dot_general(a, b, (((1,), (0,)), ((), ())), preferred_element_type=F32)


def matmul_nt(a, b):
    return lax.dot_general(a, b, (((1,), (1,)), ((), ())), preferred_element_type=F32)


def tap_mask(lanes, plane, columns, row_step, col_step):
    lane = iota((1, lanes), 1)
    column = lax.rem(lane, columns) - col_step
    row = lax.div(lax.rem(lane, plane), columns) - row_step
    rows = plane // columns
    inside = (column >= 0) & (column < columns) & (row >= 0) & (row < rows)
    return jnp.where(inside, 1.0, 0.0).astype(BF)


def rolled(value, shift):
    size = value.shape[1]
    shift = shift % size
    return value if shift == 0 else pltpu.roll(value, shift, 1)


def kernel(
    sizes,
    seed, saved, fine_pre, coarse_pre, pooled, fine_w, coarse_w,
    out, fine_all, coarse_all,
    fine_cat, coarse_cat, pre_rows, pool_rows, pre_ext, grad_ext, pool_ext, pool_out,
    coarse_gate, coarse_x, fine_cols, coarse_cols, parts, arrived,
    row_send, row_recv, halo_send, halo_recv, step_send, step_recv, sum_send, sum_recv,
    all_send, all_recv,
):
    segments, n, channels, depth, plane, per, chunks = sizes
    cw = plane // 4
    cdepth = depth // 2
    own = depth * plane
    row_len = coarse_pre.shape[1]
    s = lax.axis_index("segment")
    v = lax.axis_index("vol")
    has_left, has_right = v > 0, v < n - 1
    last = s == segments - 1

    def put(src, dst, send, recv, segment, vol):
        return pltpu.make_async_remote_copy(
            src_ref=src, dst_ref=dst, send_sem=send, recv_sem=recv,
            device_id=(segment, vol), device_id_type=pl.DeviceIdType.MESH,
        )

    barrier = pltpu.get_barrier_semaphore()

    def greet(off, carry):
        pl.semaphore_signal(
            barrier, inc=1, device_id=(s, lax.rem(v + off, n)),
            device_id_type=pl.DeviceIdType.MESH,
        )
        return carry

    lax.fori_loop(1, n, greet, 0)
    for up in (-1, 1):
        for side in (-1, 0, 1):
            there = (s + up >= 0) & (s + up < segments) & (v + side >= 0) & (v + side < n)

            @pl.when(there)
            def _(up=up, side=side):
                pl.semaphore_signal(
                    barrier, inc=1, device_id=(s + up, v + side),
                    device_id_type=pl.DeviceIdType.MESH,
                )

    ups = jnp.where(s > 0, 1, 0) + jnp.where(last, 0, 1)
    sides = 1 + jnp.where(has_left, 1, 0) + jnp.where(has_right, 1, 0)
    pl.semaphore_wait(barrier, n - 1 + ups * sides)

    to_left = put(
        fine_pre.at[:, 0:plane], pre_ext.at[:, plane + own:2 * plane + own],
        halo_send.at[0], halo_recv.at[0], s, v - 1,
    )
    to_right = put(
        fine_pre.at[:, own - plane:own], pre_ext.at[:, 0:plane],
        halo_send.at[1], halo_recv.at[1], s, v + 1,
    )

    def row_copy(which, off):
        src, dst = ((coarse_pre, pre_rows), (pooled, pool_rows))[which]
        return put(
            src, dst.at[v], row_send.at[which, off], row_recv.at[which, v],
            s, lax.rem(v + off, n),
        )

    def send_rows(which):
        def body(off, carry):
            row_copy(which, off).start()
            return carry

        lax.fori_loop(1, n, body, 0)

    def wait_rows(which):
        src, dst = ((coarse_pre, pre_rows), (pooled, pool_rows))[which]

        def body(off, carry):
            u = lax.rem(v + off, n)
            put(src, dst.at[u], row_send.at[which, off], row_recv.at[which, u], s, u).wait_recv()
            return carry

        lax.fori_loop(1, n, body, 0)

    fine_lane = iota((1, own), 1)
    pool_target = (
        lax.div(fine_lane, 2 * plane) * cw
        + lax.div(lax.rem(fine_lane, plane), 2 * XL) * HX
        + lax.div(lax.rem(fine_lane, XL), 2)
    )
    pool_matrix = jnp.where(iota((cdepth * cw, own), 0) == pool_target, 1.0, 0.0).astype(BF)

    def step_copies(src, turn, segment):
        def step(which, a, b, vol):
            return put(a, b, step_send.at[turn, which], step_recv.at[which], segment, vol)

        block = pool_out.at[turn]
        return (
            step(0, src, grad_ext.at[:, plane:plane + own], v),
            step(1, src.at[:, 0:plane], grad_ext.at[:, plane + own:2 * plane + own], v - 1),
            step(2, src.at[:, own - plane:own], grad_ext.at[:, 0:plane], v + 1),
            step(3, block, pool_ext.at[1], v),
            step(4, block, pool_ext.at[2], v - 1),
            step(5, block, pool_ext.at[0], v + 1),
        )

    def guarded(copies, act, with_own):
        if with_own:
            act(copies[3])
            act(copies[0])

        @pl.when(has_left)
        def _():
            act(copies[4])
            act(copies[1])

        @pl.when(has_right)
        def _():
            act(copies[5])
            act(copies[2])

    @pl.when(last)
    def _():
        pool_out[0] = matmul_nt(seed[...], pool_matrix).astype(BF)
        guarded(step_copies(seed, 0, s), lambda c: c.start(), False)
        grad_ext[:, plane:plane + own] = seed[...]
        pool_ext[1] = pool_out[0]

    send_rows(0)

    @pl.when(has_left)
    def _():
        to_left.start()

    @pl.when(has_right)
    def _():
        to_right.start()

    send_rows(1)

    for k in range(TAPS):
        lanes = slice(k * channels, (k + 1) * channels)
        coarse_cat[:, lanes] = coarse_w[k]
        fine_cat[:, lanes] = fine_w[k]
    pre_ext[:, plane:plane + own] = fine_pre[...]
    pre_rows[v] = coarse_pre[...]
    pool_rows[v] = pooled[...]

    @pl.when(v == 0)
    def _():
        pre_ext[:, 0:plane] = jnp.zeros((channels, plane), BF)
        grad_ext[:, 0:plane] = jnp.zeros((channels, plane), BF)
        pool_ext[0] = jnp.zeros(pool_ext.shape[1:], BF)

    @pl.when(v == n - 1)
    def _():
        pre_ext[:, plane + own:2 * plane + own] = jnp.zeros((channels, plane), BF)
        grad_ext[:, plane + own:2 * plane + own] = jnp.zeros((channels, plane), BF)
        pool_ext[2] = jnp.zeros(pool_ext.shape[1:], BF)

    up_lane = iota((1, plane), 1)
    up_target = lax.div(up_lane, 2 * XL) * HX + lax.div(lax.rem(up_lane, XL), 2)
    up_matrix = jnp.where(iota((cw, plane), 0) == up_target, 0.125, 0.0).astype(BF)

    def gathered(rows, first, planes, low, high):
        lane = iota((1, planes * cw), 1)
        slab = lax.div(lane, cw)
        target = (first + slab) * HX + lax.rem(lane, HX)
        target = jnp.where((slab >= low) & (slab < high), target, -1)
        inline = lax.div(lax.rem(lane, cw), HX)
        row = iota((row_len, planes * cw), 0)

        def body(u, total):
            pick = jnp.where(row == jnp.where(inline == u, target, -1), 1.0, 0.0).astype(BF)
            return total + matmul(rows[u], pick)

        return lax.fori_loop(0, n, body, jnp.zeros((channels, planes * cw), F32))

    wait_rows(0)
    reach = cdepth + 4
    coarse_gate[...] = gathered(pre_rows, v * cdepth - 2, reach, 0, reach).astype(BF)

    incoming = step_copies(out, 1, s)

    @pl.when(jnp.logical_not(last))
    def _():
        incoming[3].wait_recv()
        incoming[0].wait_recv()

    @pl.when(has_left)
    def _():
        incoming[5].wait_recv()
        incoming[2].wait_recv()

    @pl.when(has_right)
    def _():
        incoming[4].wait_recv()
        incoming[1].wait_recv()

    side = pool_ext.shape[2]
    near = jnp.concatenate(
        [pool_ext[0][:, side - 2 * cw:], pool_ext[1], pool_ext[2][:, :2 * cw]], axis=1
    )
    coarse_gz = jnp.where(coarse_gate[...] > 0, near, jnp.zeros_like(near))
    wide = (cdepth + 2) * cw
    for row_step in (-1, 0, 1):
        for col_step in (-1, 0, 1):
            mask = tap_mask(wide, cw, HX, row_step, col_step)
            for outer in (-1, 0, 1):
                k = (outer + 1) * 9 + (row_step + 1) * 3 + col_step + 1
                moved = rolled(coarse_gz, outer * cw + row_step * HX + col_step - cw)
                coarse_cols[k * channels:(k + 1) * channels, :] = moved[:, :wide] * mask
    coarse_back = matmul(coarse_cat[...], coarse_cols[...]).astype(BF)

    pieces = []
    for p in range(depth + 2):
        j = (p + 1) // 2
        lanes = slice(p * plane, (p + 1) * plane)
        if p and j == p // 2:
            spread = pieces[-1][1]
        else:
            spread = matmul(coarse_back[:, j * cw:(j + 1) * cw], up_matrix)
        pieces.append((None, spread))

    @pl.when(has_left)
    def _():
        to_right.wait_recv()

    @pl.when(has_right)
    def _():
        to_left.wait_recv()

    gz = []
    for p in range(depth + 2):
        lanes = slice(p * plane, (p + 1) * plane)
        grad = grad_ext[:, lanes].astype(F32) + pieces[p][1]
        gz.append(jnp.where(pre_ext[:, lanes].astype(F32) > 0, grad, 0.0).astype(BF))
    for row_step in (-1, 0, 1):
        for col_step in (-1, 0, 1):
            mask = tap_mask(plane, plane, XL, row_step, col_step)
            r = (row_step + 1) * 3 + col_step + 1
            for p in range(depth + 2):
                fine_cols[r * channels:(r + 1) * channels, p * plane:(p + 1) * plane] = (
                    rolled(gz[p], row_step * XL + col_step) * mask
                )
    group = 9 * channels
    total = grad_ext[:, plane:plane + own].astype(F32)
    for outer in range(3):
        total = total + matmul(
            fine_cat[:, outer * group:(outer + 1) * group],
            fine_cols[:, (2 - outer) * plane:(2 - outer) * plane + own],
        )
    out[...] = total.astype(BF)

    @pl.when(s > 0)
    def _():
        pool_out[1] = matmul_nt(out[...], pool_matrix).astype(BF)
        guarded(step_copies(out, 1, s - 1), lambda c: c.start(), True)

    def place(which, k, value):
        at = (k % per) * channels
        parts[which, k // per, :, at:at + channels] = value

    def chunk_of(which, vol):
        return vol if which == 0 else n - 1 - vol

    def sum_copy(which, off, vol_from, vol_to, chunk):
        return put(
            parts.at[which, chunk], arrived.at[which, vol_from],
            sum_send.at[which, off], sum_recv.at[which, vol_from], s, vol_to,
        )

    def start_sums(which):
        for k in range(TAPS, chunks * per):
            place(which, k, jnp.zeros((channels, channels), BF))

        def body(off, carry):
            t = lax.rem(v + off, n)
            chunk = chunk_of(which, t)

            @pl.when(chunk < chunks)
            def _():
                sum_copy(which, off, v, t, chunk).start()

            return carry

        lax.fori_loop(1, n, body, 0)

    for outer in range(3):
        grads = matmul_nt(
            saved[...], fine_cols[:, (2 - outer) * plane:(2 - outer) * plane + own]
        ).astype(BF)
        for r in range(9):
            place(0, outer * 9 + r, grads[:, r * channels:(r + 1) * channels])
    start_sums(0)

    wait_rows(1)
    coarse_x[...] = gathered(
        pool_rows, v * cdepth - 1, cdepth + 2, 1, 1 + cdepth
    ).astype(BF)
    grads = matmul_nt(coarse_x[...], coarse_cols[...]).astype(BF)
    for k in range(TAPS):
        place(1, k, grads[:, k * channels:(k + 1) * channels])
    start_sums(1)

    collected = (fine_all, coarse_all)

    def all_copy(which, off, chunk, vol_to):
        return put(
            collected[which].at[chunk], collected[which].at[chunk],
            all_send.at[which, off], all_recv.at[which, chunk], s, vol_to,
        )

    for which in (0, 1):
        mine = chunk_of(which, v)

        @pl.when(mine < chunks)
        def _(which=which, mine=mine):
            def add(off, carry):
                u = lax.rem(v + off, n)
                sum_copy(which, off, u, u, mine).wait_recv()
                return carry + arrived[which, u].astype(F32)

            whole = lax.fori_loop(1, n, add, parts[which, mine].astype(F32))
            collected[which][mine] = whole.astype(BF)

            def hand(off, carry):
                all_copy(which, off, mine, lax.rem(v + off, n)).start()
                return carry

            lax.fori_loop(1, n, hand, 0)

    for which in (0, 1):
        mine = chunk_of(which, v)

        def rest(off, carry, which=which, mine=mine):
            t = lax.rem(v + off, n)
            row_copy(which, off).wait_send()
            chunk = chunk_of(which, t)

            @pl.when(chunk < chunks)
            def _():
                sum_copy(which, off, v, t, chunk).wait_send()
                all_copy(which, off, chunk, t).wait_recv()

            @pl.when(mine < chunks)
            def _():
                all_copy(which, off, mine, t).wait_send()

            return carry

        lax.fori_loop(1, n, rest, 0)

    @pl.when(has_left)
    def _():
        to_left.wait_send()

    @pl.when(has_right)
    def _():
        to_right.wait_send()

    @pl.when(last)
    def _():
        guarded(step_copies(seed, 0, s), lambda c: c.wait_send(), False)

    @pl.when(s > 0)
    def _():
        guarded(step_copies(out, 1, s - 1), lambda c: c.wait_send(), True)


def on_device(
    cotangent, labels, class_weight, inputs, fine_pre, pooled, coarse_pre,
    fine_filters, coarse_filters,
):
    segments = lax.axis_size("segment")
    n = lax.axis_size("vol")
    channels, depth, plane = inputs.shape[1:]
    own = depth * plane
    cw = plane // 4
    cdepth = depth // 2
    row_len = pooled.shape[2] * pooled.shape[3]
    per = -(-TAPS // n)
    chunks = -(-TAPS // per)
    cell_weight = jnp.zeros(labels.shape, F32)
    for index in range(class_weight.shape[0]):
        cell_weight = cell_weight + jnp.where(labels == index, class_weight[index], 0.0)
    seed = (cotangent.astype(F32) * cell_weight[None]).astype(BF).reshape(channels, own)
    sizes = (segments, n, channels, depth, plane, per, chunks)
    width = TAPS * channels
    chunk_shape = (channels, per * channels)
    vmem = pl.BlockSpec(memory_space=pltpu.VMEM)
    dma = pltpu.SemaphoreType.DMA
    grad, fine_all, coarse_all = pl.pallas_call(
        functools.partial(kernel, sizes),
        out_shape=(
            jax.ShapeDtypeStruct((channels, own), BF),
            jax.ShapeDtypeStruct((chunks, *chunk_shape), BF),
            jax.ShapeDtypeStruct((chunks, *chunk_shape), BF),
        ),
        in_specs=[vmem] * 7,
        out_specs=(vmem, vmem, vmem),
        scratch_shapes=[
            pltpu.VMEM((channels, width), BF),
            pltpu.VMEM((channels, width), BF),
            pltpu.VMEM((n, channels, row_len), BF),
            pltpu.VMEM((n, channels, row_len), BF),
            pltpu.VMEM((channels, own + 2 * plane), BF),
            pltpu.VMEM((channels, own + 2 * plane), BF),
            pltpu.VMEM((3, channels, cdepth * cw), BF),
            pltpu.VMEM((2, channels, cdepth * cw), BF),
            pltpu.VMEM((channels, (cdepth + 4) * cw), BF),
            pltpu.VMEM((channels, (cdepth + 2) * cw), BF),
            pltpu.VMEM((9 * channels, own + 2 * plane), BF),
            pltpu.VMEM((width, (cdepth + 2) * cw), BF),
            pltpu.VMEM((2, chunks, *chunk_shape), BF),
            pltpu.VMEM((2, n, *chunk_shape), BF),
            dma((2, n)), dma((2, n)), dma((2,)), dma((2,)), dma((2, 6)), dma((6,)),
            dma((2, n)), dma((2, n)), dma((2, n)), dma((2, chunks)),
        ],
        compiler_params=pltpu.CompilerParams(
            collective_id=0, has_side_effects=True, vmem_limit_bytes=60 * 1024 * 1024
        ),
    )(
        seed,
        inputs[0].reshape(channels, own),
        fine_pre[0].reshape(channels, own),
        coarse_pre[0].reshape(channels, row_len),
        pooled[0].reshape(channels, row_len),
        fine_filters[0],
        coarse_filters[0],
    )

    def finish(gathered, cells):
        taps = gathered.reshape(chunks, channels, per, channels).transpose(0, 2, 1, 3)
        taps = taps.reshape(chunks * per, channels, channels)[:TAPS]
        return (taps.astype(F32) * (1.0 / math.sqrt(cells)))[None]

    cells = own * n
    return (
        grad.reshape(1, channels, depth, plane),
        finish(fine_all, cells),
        finish(coarse_all, cells // 8),
    )


def solution(mesh):
    return jax.shard_map(
        on_device,
        mesh=mesh,
        in_specs=(
            P(None, "vol", None),
            P("vol", None),
            P(),
            P("segment", None, "vol", None),
            P("segment", None, "vol", None),
            P("segment", None, "vol", None),
            P("segment", None, "vol", None),
            P("segment", None, None, None),
            P("segment", None, None, None),
        ),
        out_specs=(
            P("segment", None, "vol", None),
            P("segment", None, None, None),
            P("segment", None, None, None),
        ),
        check_vma=False,
    )
```

```python
import functools
import math

import jax
import jax.numpy as jnp
from jax import lax
from jax.experimental import pallas as pl
from jax.experimental.pallas import tpu as pltpu
from jax.sharding import PartitionSpec as P

XL = 16
HX = XL // 2
TAPS = 27
BF = jnp.bfloat16
F32 = jnp.float32


def iota(shape, dim):
    return lax.broadcasted_iota(jnp.int32, shape, dim)


def matmul(a, b):
    return lax.dot_general(a, b, (((1,), (0,)), ((), ())), preferred_element_type=F32)


def matmul_nt(a, b):
    return lax.dot_general(a, b, (((1,), (1,)), ((), ())), preferred_element_type=F32)


def tap_mask(lanes, plane, columns, row_step, col_step):
    lane = iota((1, lanes), 1)
    column = lax.rem(lane, columns) - col_step
    row = lax.div(lax.rem(lane, plane), columns) - row_step
    rows = plane // columns
    inside = (column >= 0) & (column < columns) & (row >= 0) & (row < rows)
    return jnp.where(inside, 1.0, 0.0).astype(BF)


def rolled(value, shift):
    size = value.shape[1]
    shift = shift % size
    return value if shift == 0 else pltpu.roll(value, shift, 1)


def kernel(
    sizes,
    class_weight, cotangent, labels, saved, fine_pre, coarse_pre, pooled, fine_w, coarse_w,
    out, fine_out, coarse_out,
    seed, collected, fine_cat, coarse_cat, pre_rows, pool_rows, pre_ext, grad_ext, pool_ext, pool_out,
    coarse_gate, coarse_x, fine_cols, coarse_cols, parts, arrived,
    row_send, row_recv, halo_send, halo_recv, step_send, step_recv, sum_send, sum_recv,
    all_send, all_recv, turn_sem,
):
    segments, n, channels, depth, plane, per, chunks, scales = sizes
    cw = plane // 4
    cdepth = depth // 2
    own = depth * plane
    row_len = coarse_pre.shape[1]
    s = lax.axis_index("segment")
    v = lax.axis_index("vol")
    has_left, has_right = v > 0, v < n - 1
    last = s == segments - 1

    def put(src, dst, send, recv, segment, vol):
        return pltpu.make_async_remote_copy(
            src_ref=src, dst_ref=dst, send_sem=send, recv_sem=recv,
            device_id=(segment, vol), device_id_type=pl.DeviceIdType.MESH,
        )

    barrier = pltpu.get_barrier_semaphore()

    def greet(off, carry):
        pl.semaphore_signal(
            barrier, inc=1, device_id=(s, lax.rem(v + off, n)),
            device_id_type=pl.DeviceIdType.MESH,
        )
        return carry

    lax.fori_loop(1, n, greet, 0)
    for up in (-1, 1):
        for side in (-1, 0, 1):
            there = (s + up >= 0) & (s + up < segments) & (v + side >= 0) & (v + side < n)

            @pl.when(there)
            def _(up=up, side=side):
                pl.semaphore_signal(
                    barrier, inc=1, device_id=(s + up, v + side),
                    device_id_type=pl.DeviceIdType.MESH,
                )

    ups = jnp.where(s > 0, 1, 0) + jnp.where(last, 0, 1)
    sides = 1 + jnp.where(has_left, 1, 0) + jnp.where(has_right, 1, 0)
    pl.semaphore_wait(barrier, n - 1 + ups * sides)

    to_left = put(
        fine_pre.at[0], pre_ext.at[depth + 1],
        halo_send.at[0], halo_recv.at[0], s, v - 1,
    )
    to_right = put(
        fine_pre.at[depth - 1], pre_ext.at[0],
        halo_send.at[1], halo_recv.at[1], s, v + 1,
    )

    def row_copy(which, off):
        src, dst = ((coarse_pre, pre_rows), (pooled, pool_rows))[which]
        return put(
            src, dst.at[v], row_send.at[which, off], row_recv.at[which, v],
            s, lax.rem(v + off, n),
        )

    def send_rows(which):
        def body(off, carry):
            row_copy(which, off).start()
            return carry

        lax.fori_loop(1, n, body, 0)

    def wait_rows(which):
        src, dst = ((coarse_pre, pre_rows), (pooled, pool_rows))[which]

        def body(off, carry):
            u = lax.rem(v + off, n)
            put(src, dst.at[u], row_send.at[which, off], row_recv.at[which, u], s, u).wait_recv()
            return carry

        lax.fori_loop(1, n, body, 0)

    fine_lane = iota((1, own), 1)
    pool_target = (
        lax.div(fine_lane, 2 * plane) * cw
        + lax.div(lax.rem(fine_lane, plane), 2 * XL) * HX
        + lax.div(lax.rem(fine_lane, XL), 2)
    )
    pool_matrix = jnp.where(iota((cdepth * cw, own), 0) == pool_target, 1.0, 0.0).astype(BF)

    def step_copies(src, turn, segment):
        def step(which, a, b, vol):
            return put(a, b, step_send.at[turn, which], step_recv.at[which], segment, vol)

        block = pool_out.at[turn]
        return (
            step(0, src, grad_ext.at[1:depth + 1], v),
            step(1, src.at[0], grad_ext.at[depth + 1], v - 1),
            step(2, src.at[depth - 1], grad_ext.at[0], v + 1),
            step(3, block, pool_ext.at[1], v),
            step(4, block, pool_ext.at[2], v - 1),
            step(5, block, pool_ext.at[0], v + 1),
        )

    def guarded(copies, act, with_own):
        @pl.when(has_left)
        def _():
            act(copies[4])

        @pl.when(has_right)
        def _():
            act(copies[5])

        if with_own:
            act(copies[3])

        @pl.when(has_left)
        def _():
            act(copies[1])

        @pl.when(has_right)
        def _():
            act(copies[2])

        if with_own:
            act(copies[0])

    def joined(ref):
        return jnp.concatenate([ref[p] for p in range(depth)], axis=1)

    def send_saved():
        send_rows(0)

        @pl.when(has_left)
        def _():
            to_left.start()

        @pl.when(has_right)
        def _():
            to_right.start()

    @pl.when(last)
    def _():
        send_rows(0)
        for p in range(depth):
            label = labels[p:p + 1, :]
            weight = jnp.zeros(label.shape, F32)
            for index in range(class_weight.shape[0]):
                weight = weight + jnp.where(label == index, class_weight[index], 0.0)
            block = (cotangent[p].astype(F32) * weight).astype(BF)
            seed[p] = block
            grad_ext[p + 1] = block
        pool_out[0] = matmul_nt(joined(seed), pool_matrix).astype(BF)
        guarded(step_copies(seed, 0, s), lambda c: c.start(), False)
        pool_ext[1] = pool_out[0]

        @pl.when(has_left)
        def _():
            to_left.start()

        @pl.when(has_right)
        def _():
            to_right.start()

    for k in range(TAPS):
        lanes = slice(k * channels, (k + 1) * channels)
        coarse_cat[:, lanes] = coarse_w[k]
        fine_cat[:, lanes] = fine_w[k]
    for p in range(depth):
        pre_ext[p + 1] = fine_pre[p]
    pre_rows[v] = coarse_pre[...]
    pool_rows[v] = pooled[...]

    @pl.when(v == 0)
    def _():
        pre_ext[0] = jnp.zeros((channels, plane), BF)
        grad_ext[0] = jnp.zeros((channels, plane), BF)
        pool_ext[0] = jnp.zeros(pool_ext.shape[1:], BF)

    @pl.when(v == n - 1)
    def _():
        pre_ext[depth + 1] = jnp.zeros((channels, plane), BF)
        grad_ext[depth + 1] = jnp.zeros((channels, plane), BF)
        pool_ext[2] = jnp.zeros(pool_ext.shape[1:], BF)

    up_lane = iota((1, plane), 1)
    up_target = lax.div(up_lane, 2 * XL) * HX + lax.div(lax.rem(up_lane, XL), 2)
    up_matrix = jnp.where(iota((cw, plane), 0) == up_target, 0.125, 0.0).astype(BF)

    def gathered(rows, first, planes, low, high):
        lane = iota((1, planes * cw), 1)
        slab = lax.div(lane, cw)
        target = (first + slab) * HX + lax.rem(lane, HX)
        target = jnp.where((slab >= low) & (slab < high), target, -1)
        inline = lax.div(lax.rem(lane, cw), HX)
        row = iota((row_len, planes * cw), 0)

        def body(u, total):
            pick = jnp.where(row == jnp.where(inline == u, target, -1), 1.0, 0.0).astype(BF)
            return total + matmul(rows[u], pick)

        return lax.fori_loop(0, n, body, jnp.zeros((channels, planes * cw), F32))

    @pl.when(jnp.logical_not(last))
    def _():
        pl.semaphore_wait(turn_sem, 1)
        send_saved()

    wait_rows(0)

    @pl.when(s > 0)
    def _():
        pl.semaphore_signal(
            turn_sem, inc=1, device_id=(s - 1, v), device_id_type=pl.DeviceIdType.MESH
        )

    send_rows(1)
    reach = cdepth + 4
    coarse_gate[...] = gathered(pre_rows, v * cdepth - 2, reach, 0, reach).astype(BF)

    def take_pooled():
        wait_rows(1)
        coarse_x[...] = gathered(
            pool_rows, v * cdepth - 1, cdepth + 2, 1, 1 + cdepth
        ).astype(BF)

    @pl.when(jnp.logical_not(last))
    def _():
        take_pooled()

    incoming = step_copies(out, 1, s)

    def wait_incoming(middle, left, right):
        @pl.when(jnp.logical_not(last))
        def _():
            incoming[middle].wait_recv()

        @pl.when(has_left)
        def _():
            incoming[left].wait_recv()

        @pl.when(has_right)
        def _():
            incoming[right].wait_recv()

    wait_incoming(3, 5, 4)

    def place(which, k, value):
        at = (k % per) * channels
        parts[which, k // per, :, at:at + channels] = value

    def chunk_of(which, vol):
        return vol if which == 0 else n - 1 - vol

    def sum_copy(which, off, vol_from, vol_to, chunk):
        return put(
            parts.at[which, chunk], arrived.at[which, vol_from],
            sum_send.at[which, off], sum_recv.at[which, vol_from], s, vol_to,
        )

    def start_sums(which):
        for k in range(TAPS, chunks * per):
            place(which, k, jnp.zeros((channels, channels), BF))

        def body(off, carry):
            t = lax.rem(v + off, n)
            chunk = chunk_of(which, t)

            @pl.when(chunk < chunks)
            def _():
                sum_copy(which, off, v, t, chunk).start()

            return carry

        lax.fori_loop(1, n, body, 0)

    def fine_sums():
        rows = joined(saved)
        for outer in range(3):
            grads = matmul_nt(
                rows, fine_cols[:, (2 - outer) * plane:(2 - outer) * plane + own]
            ).astype(BF)
            for r in range(9):
                place(0, outer * 9 + r, grads[:, r * channels:(r + 1) * channels])
        start_sums(0)

    def coarse_sums():
        grads = matmul_nt(coarse_x[...], coarse_cols[...]).astype(BF)
        for k in range(TAPS):
            place(1, k, grads[:, k * channels:(k + 1) * channels])
        start_sums(1)

    side = pool_ext.shape[2]
    near = jnp.concatenate(
        [pool_ext[0][:, side - 2 * cw:], pool_ext[1], pool_ext[2][:, :2 * cw]], axis=1
    )
    coarse_gz = jnp.where(coarse_gate[...] > 0, near, jnp.zeros_like(near))
    wide = (cdepth + 2) * cw
    for row_step in (-1, 0, 1):
        for col_step in (-1, 0, 1):
            mask = tap_mask(wide, cw, HX, row_step, col_step)
            for outer in (-1, 0, 1):
                k = (outer + 1) * 9 + (row_step + 1) * 3 + col_step + 1
                moved = rolled(coarse_gz, outer * cw + row_step * HX + col_step - cw)
                coarse_cols[k * channels:(k + 1) * channels, :] = moved[:, :wide] * mask
    @pl.when(s == 0)
    def _():
        coarse_sums()

    coarse_back = matmul(coarse_cat[...], coarse_cols[...]).astype(BF)

    pieces = []
    for p in range(depth + 2):
        j = (p + 1) // 2
        if p and j == p // 2:
            spread = pieces[-1]
        else:
            spread = matmul(coarse_back[:, j * cw:(j + 1) * cw], up_matrix)
        pieces.append(spread)

    @pl.when(has_left)
    def _():
        to_right.wait_recv()

    @pl.when(has_right)
    def _():
        to_left.wait_recv()

    wait_incoming(0, 2, 1)
    gz = []
    for p in range(depth + 2):
        grad = grad_ext[p].astype(F32) + pieces[p]
        gz.append(jnp.where(pre_ext[p].astype(F32) > 0, grad, 0.0).astype(BF))
    for row_step in (-1, 0, 1):
        for col_step in (-1, 0, 1):
            mask = tap_mask(plane, plane, XL, row_step, col_step)
            r = (row_step + 1) * 3 + col_step + 1
            for p in range(depth + 2):
                fine_cols[r * channels:(r + 1) * channels, p * plane:(p + 1) * plane] = (
                    rolled(gz[p], row_step * XL + col_step) * mask
                )
    @pl.when(s == 0)
    def _():
        fine_sums()

    group = 9 * channels
    total = jnp.concatenate([grad_ext[p + 1].astype(F32) for p in range(depth)], axis=1)
    for outer in range(3):
        total = total + matmul(
            fine_cat[:, outer * group:(outer + 1) * group],
            fine_cols[:, (2 - outer) * plane:(2 - outer) * plane + own],
        )
    for p in range(depth):
        out[p] = total[:, p * plane:(p + 1) * plane].astype(BF)

    @pl.when(s > 0)
    def _():
        pool_out[1] = matmul_nt(joined(out), pool_matrix).astype(BF)
        guarded(step_copies(out, 1, s - 1), lambda c: c.start(), True)

    @pl.when(s > 0)
    def _():
        fine_sums()

        @pl.when(last)
        def _():
            take_pooled()

        coarse_sums()

    def all_copy(which, off, chunk, vol_to):
        return put(
            collected.at[which, chunk], collected.at[which, chunk],
            all_send.at[which, off], all_recv.at[which, chunk], s, vol_to,
        )

    for which in (1, 0):
        mine = chunk_of(which, v)

        @pl.when(mine < chunks)
        def _(which=which, mine=mine):
            def add(off, carry):
                u = lax.rem(v + off, n)
                sum_copy(which, off, u, u, mine).wait_recv()
                return carry + arrived[which, u].astype(F32)

            whole = lax.fori_loop(1, n, add, parts[which, mine].astype(F32))
            collected[which, mine] = whole.astype(BF)

            def hand(off, carry):
                all_copy(which, off, mine, lax.rem(v + off, n)).start()
                return carry

            lax.fori_loop(1, n, hand, 0)

    for which in (1, 0):
        ref, scale = ((fine_out, scales[0]), (coarse_out, scales[1]))[which]
        for chunk in range(chunks):
            @pl.when(chunk_of(which, v) != chunk)
            def _(which=which, chunk=chunk):
                all_copy(which, 1, chunk, v).wait_recv()

            for k in range(chunk * per, min(TAPS, (chunk + 1) * per)):
                at = (k % per) * channels
                ref[k] = collected[which, chunk, :, at:at + channels].astype(F32) * scale

    for which in (0, 1):
        mine = chunk_of(which, v)

        def rest(off, carry, which=which, mine=mine):
            t = lax.rem(v + off, n)
            row_copy(which, off).wait_send()
            chunk = chunk_of(which, t)

            @pl.when(chunk < chunks)
            def _():
                sum_copy(which, off, v, t, chunk).wait_send()

            @pl.when(mine < chunks)
            def _():
                all_copy(which, off, mine, t).wait_send()

            return carry

        lax.fori_loop(1, n, rest, 0)

    @pl.when(has_left)
    def _():
        to_left.wait_send()

    @pl.when(has_right)
    def _():
        to_right.wait_send()

    @pl.when(last)
    def _():
        guarded(step_copies(seed, 0, s), lambda c: c.wait_send(), False)

    @pl.when(s > 0)
    def _():
        guarded(step_copies(out, 1, s - 1), lambda c: c.wait_send(), True)


def on_device(
    cotangent, labels, class_weight, inputs, fine_pre, pooled, coarse_pre,
    fine_filters, coarse_filters,
):
    segments = lax.axis_size("segment")
    n = lax.axis_size("vol")
    channels, depth, plane = inputs.shape[1:]
    own = depth * plane
    cw = plane // 4
    cdepth = depth // 2
    row_len = pooled.shape[2] * pooled.shape[3]
    per = -(-TAPS // n)
    chunks = -(-TAPS // per)
    cells = own * n
    scales = (1.0 / math.sqrt(cells), 1.0 / math.sqrt(cells // 8))
    sizes = (segments, n, channels, depth, plane, per, chunks, scales)
    width = TAPS * channels
    chunk_shape = (channels, per * channels)
    vmem = pl.BlockSpec(memory_space=pltpu.VMEM)
    dma = pltpu.SemaphoreType.DMA
    grad, fine_grads, coarse_grads = pl.pallas_call(
        functools.partial(kernel, sizes),
        out_shape=(
            jax.ShapeDtypeStruct((depth, channels, plane), BF),
            jax.ShapeDtypeStruct((TAPS, channels, channels), F32),
            jax.ShapeDtypeStruct((TAPS, channels, channels), F32),
        ),
        in_specs=[pl.BlockSpec(memory_space=pltpu.SMEM)] + [vmem] * 8,
        out_specs=(vmem, vmem, vmem),
        scratch_shapes=[
            pltpu.VMEM((depth, channels, plane), BF),
            pltpu.VMEM((2, chunks, *chunk_shape), BF),
            pltpu.VMEM((channels, width), BF),
            pltpu.VMEM((channels, width), BF),
            pltpu.VMEM((n, channels, row_len), BF),
            pltpu.VMEM((n, channels, row_len), BF),
            pltpu.VMEM((depth + 2, channels, plane), BF),
            pltpu.VMEM((depth + 2, channels, plane), BF),
            pltpu.VMEM((3, channels, cdepth * cw), BF),
            pltpu.VMEM((2, channels, cdepth * cw), BF),
            pltpu.VMEM((channels, (cdepth + 4) * cw), BF),
            pltpu.VMEM((channels, (cdepth + 2) * cw), BF),
            pltpu.VMEM((9 * channels, own + 2 * plane), BF),
            pltpu.VMEM((width, (cdepth + 2) * cw), BF),
            pltpu.VMEM((2, chunks, *chunk_shape), BF),
            pltpu.VMEM((2, n, *chunk_shape), BF),
            dma((2, n)), dma((2, n)), dma((2,)), dma((2,)), dma((2, 6)), dma((6,)),
            dma((2, n)), dma((2, n)), dma((2, n)), dma((2, chunks)),
            pltpu.SemaphoreType.REGULAR,
        ],
        compiler_params=pltpu.CompilerParams(
            collective_id=0, has_side_effects=True, vmem_limit_bytes=60 * 1024 * 1024
        ),
    )(
        class_weight,
        cotangent.transpose(1, 0, 2),
        labels,
        inputs[0].transpose(1, 0, 2),
        fine_pre[0].transpose(1, 0, 2),
        coarse_pre[0].reshape(channels, row_len),
        pooled[0].reshape(channels, row_len),
        fine_filters[0],
        coarse_filters[0],
    )

    return (grad.transpose(1, 0, 2)[None], fine_grads[None], coarse_grads[None])


def solution(mesh):
    return jax.shard_map(
        on_device,
        mesh=mesh,
        in_specs=(
            P(None, "vol", None),
            P("vol", None),
            P(),
            P("segment", None, "vol", None),
            P("segment", None, "vol", None),
            P("segment", None, "vol", None),
            P("segment", None, "vol", None),
            P("segment", None, None, None),
            P("segment", None, None, None),
        ),
        out_specs=(
            P("segment", None, "vol", None),
            P("segment", None, None, None),
            P("segment", None, None, None),
        ),
        check_vma=False,
    )
```

```python
import functools
import math

import jax
import jax.numpy as jnp
from jax import lax
from jax.experimental import pallas as pl
from jax.experimental.pallas import tpu as pltpu
from jax.sharding import PartitionSpec as P

XL = 16
HX = XL // 2
TAPS = 27
BF = jnp.bfloat16
F32 = jnp.float32


def iota(shape, dim):
    return lax.broadcasted_iota(jnp.int32, shape, dim)


def matmul(a, b):
    return lax.dot_general(a, b, (((1,), (0,)), ((), ())), preferred_element_type=F32)


def matmul_nt(a, b):
    return lax.dot_general(a, b, (((1,), (1,)), ((), ())), preferred_element_type=F32)


def tap_mask(lanes, plane, columns, row_step, col_step):
    lane = iota((1, lanes), 1)
    column = lax.rem(lane, columns) - col_step
    row = lax.div(lax.rem(lane, plane), columns) - row_step
    rows = plane // columns
    inside = (column >= 0) & (column < columns) & (row >= 0) & (row < rows)
    return jnp.where(inside, 1.0, 0.0).astype(BF)


def rolled(value, shift):
    size = value.shape[1]
    shift = shift % size
    return value if shift == 0 else pltpu.roll(value, shift, 1)


def kernel(
    sizes,
    class_weight, cotangent, labels, saved, fine_pre, coarse_pre, pooled, fine_w, coarse_w,
    out, collected,
    seed, fine_cat, coarse_cat, pre_rows, pool_rows, pre_ext, grad_ext, pool_ext, pool_out,
    coarse_gate, coarse_x, fine_cols, coarse_cols, parts, arrived,
    row_send, row_recv, halo_send, halo_recv, step_send, step_recv, sum_send, sum_recv,
    all_send, all_recv,
):
    segments, n, channels, depth, plane, per, chunks = sizes
    cw = plane // 4
    cdepth = depth // 2
    own = depth * plane
    row_len = coarse_pre.shape[1]
    s = lax.axis_index("segment")
    v = lax.axis_index("vol")
    has_left, has_right = v > 0, v < n - 1
    last = s == segments - 1

    def put(src, dst, send, recv, segment, vol):
        return pltpu.make_async_remote_copy(
            src_ref=src, dst_ref=dst, send_sem=send, recv_sem=recv,
            device_id=(segment, vol), device_id_type=pl.DeviceIdType.MESH,
        )

    barrier = pltpu.get_barrier_semaphore()

    def greet(off, carry):
        pl.semaphore_signal(
            barrier, inc=1, device_id=(s, lax.rem(v + off, n)),
            device_id_type=pl.DeviceIdType.MESH,
        )
        return carry

    lax.fori_loop(1, n, greet, 0)
    for up in (-1, 1):
        for side in (-1, 0, 1):
            there = (s + up >= 0) & (s + up < segments) & (v + side >= 0) & (v + side < n)

            @pl.when(there)
            def _(up=up, side=side):
                pl.semaphore_signal(
                    barrier, inc=1, device_id=(s + up, v + side),
                    device_id_type=pl.DeviceIdType.MESH,
                )

    ups = jnp.where(s > 0, 1, 0) + jnp.where(last, 0, 1)
    sides = 1 + jnp.where(has_left, 1, 0) + jnp.where(has_right, 1, 0)
    pl.semaphore_wait(barrier, n - 1 + ups * sides)

    to_left = put(
        fine_pre.at[0], pre_ext.at[depth + 1],
        halo_send.at[0], halo_recv.at[0], s, v - 1,
    )
    to_right = put(
        fine_pre.at[depth - 1], pre_ext.at[0],
        halo_send.at[1], halo_recv.at[1], s, v + 1,
    )

    def row_copy(which, off):
        src, dst = ((coarse_pre, pre_rows), (pooled, pool_rows))[which]
        return put(
            src, dst.at[v], row_send.at[which, off], row_recv.at[which, v],
            s, lax.rem(v + off, n),
        )

    def send_rows(which):
        def body(off, carry):
            row_copy(which, off).start()
            return carry

        lax.fori_loop(1, n, body, 0)

    def wait_rows(which):
        src, dst = ((coarse_pre, pre_rows), (pooled, pool_rows))[which]

        def body(off, carry):
            u = lax.rem(v + off, n)
            put(src, dst.at[u], row_send.at[which, off], row_recv.at[which, u], s, u).wait_recv()
            return carry

        lax.fori_loop(1, n, body, 0)

    fine_lane = iota((1, own), 1)
    pool_target = (
        lax.div(fine_lane, 2 * plane) * cw
        + lax.div(lax.rem(fine_lane, plane), 2 * XL) * HX
        + lax.div(lax.rem(fine_lane, XL), 2)
    )
    pool_matrix = jnp.where(iota((cdepth * cw, own), 0) == pool_target, 1.0, 0.0).astype(BF)

    def step_copies(src, turn, segment):
        def step(which, a, b, vol):
            return put(a, b, step_send.at[turn, which], step_recv.at[which], segment, vol)

        block = pool_out.at[turn]
        return (
            step(0, src, grad_ext.at[1:depth + 1], v),
            step(1, src.at[0], grad_ext.at[depth + 1], v - 1),
            step(2, src.at[depth - 1], grad_ext.at[0], v + 1),
            step(3, block, pool_ext.at[1], v),
            step(4, block, pool_ext.at[2], v - 1),
            step(5, block, pool_ext.at[0], v + 1),
        )

    def guarded(copies, act, with_own):
        @pl.when(has_left)
        def _():
            act(copies[4])

        @pl.when(has_right)
        def _():
            act(copies[5])

        if with_own:
            act(copies[3])

        @pl.when(has_left)
        def _():
            act(copies[1])

        @pl.when(has_right)
        def _():
            act(copies[2])

        if with_own:
            act(copies[0])

    def joined(ref):
        return jnp.concatenate([ref[p] for p in range(depth)], axis=1)

    send_rows(0)

    @pl.when(last)
    def _():
        for p in range(depth):
            label = labels[p:p + 1, :]
            weight = jnp.zeros(label.shape, F32)
            for index in range(class_weight.shape[0]):
                weight = weight + jnp.where(label == index, class_weight[index], 0.0)
            block = (cotangent[p].astype(F32) * weight).astype(BF)
            seed[p] = block
            grad_ext[p + 1] = block
        pool_out[0] = matmul_nt(joined(seed), pool_matrix).astype(BF)
        guarded(step_copies(seed, 0, s), lambda c: c.start(), False)
        pool_ext[1] = pool_out[0]

    @pl.when(has_left)
    def _():
        to_left.start()

    @pl.when(has_right)
    def _():
        to_right.start()

    for k in range(TAPS):
        lanes = slice(k * channels, (k + 1) * channels)
        coarse_cat[:, lanes] = coarse_w[k]
        fine_cat[:, lanes] = fine_w[k]
    for p in range(depth):
        pre_ext[p + 1] = fine_pre[p]
    pre_rows[v] = coarse_pre[...]
    pool_rows[v] = pooled[...]

    @pl.when(v == 0)
    def _():
        pre_ext[0] = jnp.zeros((channels, plane), BF)
        grad_ext[0] = jnp.zeros((channels, plane), BF)
        pool_ext[0] = jnp.zeros(pool_ext.shape[1:], BF)

    @pl.when(v == n - 1)
    def _():
        pre_ext[depth + 1] = jnp.zeros((channels, plane), BF)
        grad_ext[depth + 1] = jnp.zeros((channels, plane), BF)
        pool_ext[2] = jnp.zeros(pool_ext.shape[1:], BF)

    up_lane = iota((1, plane), 1)
    up_target = lax.div(up_lane, 2 * XL) * HX + lax.div(lax.rem(up_lane, XL), 2)
    up_matrix = jnp.where(iota((cw, plane), 0) == up_target, 0.125, 0.0).astype(BF)

    def gathered(rows, first, planes, low, high):
        lane = iota((1, planes * cw), 1)
        slab = lax.div(lane, cw)
        target = (first + slab) * HX + lax.rem(lane, HX)
        target = jnp.where((slab >= low) & (slab < high), target, -1)
        inline = lax.div(lax.rem(lane, cw), HX)
        row = iota((row_len, planes * cw), 0)

        def body(u, total):
            pick = jnp.where(row == jnp.where(inline == u, target, -1), 1.0, 0.0).astype(BF)
            return total + matmul(rows[u], pick)

        return lax.fori_loop(0, n, body, jnp.zeros((channels, planes * cw), F32))

    wait_rows(0)
    send_rows(1)
    reach = cdepth + 4
    coarse_gate[...] = gathered(pre_rows, v * cdepth - 2, reach, 0, reach).astype(BF)

    def take_pooled():
        wait_rows(1)
        coarse_x[...] = gathered(
            pool_rows, v * cdepth - 1, cdepth + 2, 1, 1 + cdepth
        ).astype(BF)

    @pl.when(jnp.logical_not(last))
    def _():
        take_pooled()

    incoming = step_copies(out, 1, s)

    def wait_incoming(middle, left, right):
        @pl.when(jnp.logical_not(last))
        def _():
            incoming[middle].wait_recv()

        @pl.when(has_left)
        def _():
            incoming[left].wait_recv()

        @pl.when(has_right)
        def _():
            incoming[right].wait_recv()

    wait_incoming(3, 5, 4)

    def place(which, k, value):
        at = (k % per) * channels
        parts[which, k // per, :, at:at + channels] = value

    def chunk_of(which, vol):
        return vol if which == 0 else n - 1 - vol

    def sum_copy(which, off, vol_from, vol_to, chunk):
        return put(
            parts.at[which, chunk], arrived.at[which, vol_from],
            sum_send.at[which, off], sum_recv.at[which, vol_from], s, vol_to,
        )

    def start_sums(which):
        for k in range(TAPS, chunks * per):
            place(which, k, jnp.zeros((channels, channels), BF))

        def body(off, carry):
            t = lax.rem(v + off, n)
            chunk = chunk_of(which, t)

            @pl.when(chunk < chunks)
            def _():
                sum_copy(which, off, v, t, chunk).start()

            return carry

        lax.fori_loop(1, n, body, 0)

    def fine_sums():
        rows = joined(saved)
        for outer in range(3):
            grads = matmul_nt(
                rows, fine_cols[:, (2 - outer) * plane:(2 - outer) * plane + own]
            ).astype(BF)
            for r in range(9):
                place(0, outer * 9 + r, grads[:, r * channels:(r + 1) * channels])
        start_sums(0)

    def coarse_sums():
        grads = matmul_nt(coarse_x[...], coarse_cols[...]).astype(BF)
        for k in range(TAPS):
            place(1, k, grads[:, k * channels:(k + 1) * channels])
        start_sums(1)

    side = pool_ext.shape[2]
    near = jnp.concatenate(
        [pool_ext[0][:, side - 2 * cw:], pool_ext[1], pool_ext[2][:, :2 * cw]], axis=1
    )
    coarse_gz = jnp.where(coarse_gate[...] > 0, near, jnp.zeros_like(near))
    wide = (cdepth + 2) * cw
    for row_step in (-1, 0, 1):
        for col_step in (-1, 0, 1):
            mask = tap_mask(wide, cw, HX, row_step, col_step)
            for outer in (-1, 0, 1):
                k = (outer + 1) * 9 + (row_step + 1) * 3 + col_step + 1
                moved = rolled(coarse_gz, outer * cw + row_step * HX + col_step - cw)
                coarse_cols[k * channels:(k + 1) * channels, :] = moved[:, :wide] * mask
    @pl.when(s == 0)
    def _():
        coarse_sums()

    coarse_back = matmul(coarse_cat[...], coarse_cols[...]).astype(BF)

    pieces = []
    for p in range(depth + 2):
        j = (p + 1) // 2
        if p and j == p // 2:
            spread = pieces[-1]
        else:
            spread = matmul(coarse_back[:, j * cw:(j + 1) * cw], up_matrix)
        pieces.append(spread)

    @pl.when(has_left)
    def _():
        to_right.wait_recv()

    @pl.when(has_right)
    def _():
        to_left.wait_recv()

    wait_incoming(0, 2, 1)
    gz = []
    for p in range(depth + 2):
        grad = grad_ext[p].astype(F32) + pieces[p]
        gz.append(jnp.where(pre_ext[p].astype(F32) > 0, grad, 0.0).astype(BF))
    for row_step in (-1, 0, 1):
        for col_step in (-1, 0, 1):
            mask = tap_mask(plane, plane, XL, row_step, col_step)
            r = (row_step + 1) * 3 + col_step + 1
            for p in range(depth + 2):
                fine_cols[r * channels:(r + 1) * channels, p * plane:(p + 1) * plane] = (
                    rolled(gz[p], row_step * XL + col_step) * mask
                )
    @pl.when(s == 0)
    def _():
        fine_sums()

    group = 9 * channels
    total = jnp.concatenate([grad_ext[p + 1].astype(F32) for p in range(depth)], axis=1)
    for outer in range(3):
        total = total + matmul(
            fine_cat[:, outer * group:(outer + 1) * group],
            fine_cols[:, (2 - outer) * plane:(2 - outer) * plane + own],
        )
    for p in range(depth):
        out[p] = total[:, p * plane:(p + 1) * plane].astype(BF)

    @pl.when(s > 0)
    def _():
        pool_out[1] = matmul_nt(joined(out), pool_matrix).astype(BF)
        guarded(step_copies(out, 1, s - 1), lambda c: c.start(), True)

    @pl.when(s > 0)
    def _():
        fine_sums()

        @pl.when(last)
        def _():
            take_pooled()

        coarse_sums()

    def all_copy(which, off, chunk, vol_to):
        return put(
            collected.at[which, chunk], collected.at[which, chunk],
            all_send.at[which, off], all_recv.at[which, chunk], s, vol_to,
        )

    for which in (1, 0):
        mine = chunk_of(which, v)

        @pl.when(mine < chunks)
        def _(which=which, mine=mine):
            def add(off, carry):
                u = lax.rem(v + off, n)
                sum_copy(which, off, u, u, mine).wait_recv()
                return carry + arrived[which, u].astype(F32)

            whole = lax.fori_loop(1, n, add, parts[which, mine].astype(F32))
            collected[which, mine] = whole.astype(BF)

            def hand(off, carry):
                all_copy(which, off, mine, lax.rem(v + off, n)).start()
                return carry

            lax.fori_loop(1, n, hand, 0)

    for which in (0, 1):
        mine = chunk_of(which, v)

        def rest(off, carry, which=which, mine=mine):
            t = lax.rem(v + off, n)
            row_copy(which, off).wait_send()
            chunk = chunk_of(which, t)

            @pl.when(chunk < chunks)
            def _():
                sum_copy(which, off, v, t, chunk).wait_send()
                all_copy(which, off, chunk, t).wait_recv()

            @pl.when(mine < chunks)
            def _():
                all_copy(which, off, mine, t).wait_send()

            return carry

        lax.fori_loop(1, n, rest, 0)

    @pl.when(has_left)
    def _():
        to_left.wait_send()

    @pl.when(has_right)
    def _():
        to_right.wait_send()

    @pl.when(last)
    def _():
        guarded(step_copies(seed, 0, s), lambda c: c.wait_send(), False)

    @pl.when(s > 0)
    def _():
        guarded(step_copies(out, 1, s - 1), lambda c: c.wait_send(), True)


def finish(per, scales, collected, fine_out, coarse_out):
    channels = fine_out.shape[1]
    for which, ref in enumerate((fine_out, coarse_out)):
        for k in range(TAPS):
            at = (k % per) * channels
            value = collected[which, k // per, :, at:at + channels]
            ref[k] = value.astype(F32) * scales[which]


def on_device(
    cotangent, labels, class_weight, inputs, fine_pre, pooled, coarse_pre,
    fine_filters, coarse_filters,
):
    segments = lax.axis_size("segment")
    n = lax.axis_size("vol")
    channels, depth, plane = inputs.shape[1:]
    own = depth * plane
    cw = plane // 4
    cdepth = depth // 2
    row_len = pooled.shape[2] * pooled.shape[3]
    per = -(-TAPS // n)
    chunks = -(-TAPS // per)
    cells = own * n
    scales = (1.0 / math.sqrt(cells), 1.0 / math.sqrt(cells // 8))
    sizes = (segments, n, channels, depth, plane, per, chunks)
    width = TAPS * channels
    chunk_shape = (channels, per * channels)
    vmem = pl.BlockSpec(memory_space=pltpu.VMEM)
    dma = pltpu.SemaphoreType.DMA
    grad, collected = pl.pallas_call(
        functools.partial(kernel, sizes),
        out_shape=(
            jax.ShapeDtypeStruct((depth, channels, plane), BF),
            jax.ShapeDtypeStruct((2, chunks, *chunk_shape), BF),
        ),
        in_specs=[pl.BlockSpec(memory_space=pltpu.SMEM)] + [vmem] * 8,
        out_specs=(vmem, vmem),
        scratch_shapes=[
            pltpu.VMEM((depth, channels, plane), BF),
            pltpu.VMEM((channels, width), BF),
            pltpu.VMEM((channels, width), BF),
            pltpu.VMEM((n, channels, row_len), BF),
            pltpu.VMEM((n, channels, row_len), BF),
            pltpu.VMEM((depth + 2, channels, plane), BF),
            pltpu.VMEM((depth + 2, channels, plane), BF),
            pltpu.VMEM((3, channels, cdepth * cw), BF),
            pltpu.VMEM((2, channels, cdepth * cw), BF),
            pltpu.VMEM((channels, (cdepth + 4) * cw), BF),
            pltpu.VMEM((channels, (cdepth + 2) * cw), BF),
            pltpu.VMEM((9 * channels, own + 2 * plane), BF),
            pltpu.VMEM((width, (cdepth + 2) * cw), BF),
            pltpu.VMEM((2, chunks, *chunk_shape), BF),
            pltpu.VMEM((2, n, *chunk_shape), BF),
            dma((2, n)), dma((2, n)), dma((2,)), dma((2,)), dma((2, 6)), dma((6,)),
            dma((2, n)), dma((2, n)), dma((2, n)), dma((2, chunks)),
        ],
        compiler_params=pltpu.CompilerParams(
            collective_id=0, has_side_effects=True, vmem_limit_bytes=60 * 1024 * 1024
        ),
    )(
        class_weight,
        cotangent.transpose(1, 0, 2),
        labels,
        inputs[0].transpose(1, 0, 2),
        fine_pre[0].transpose(1, 0, 2),
        coarse_pre[0].reshape(channels, row_len),
        pooled[0].reshape(channels, row_len),
        fine_filters[0],
        coarse_filters[0],
    )

    tap_shape = jax.ShapeDtypeStruct((TAPS, channels, channels), F32)
    fine_grads, coarse_grads = pl.pallas_call(
        functools.partial(finish, per, scales),
        out_shape=(tap_shape, tap_shape),
        in_specs=[vmem],
        out_specs=(vmem, vmem),
    )(collected)
    return (grad.transpose(1, 0, 2)[None], fine_grads[None], coarse_grads[None])


def solution(mesh):
    return jax.shard_map(
        on_device,
        mesh=mesh,
        in_specs=(
            P(None, "vol", None),
            P("vol", None),
            P(),
            P("segment", None, "vol", None),
            P("segment", None, "vol", None),
            P("segment", None, "vol", None),
            P("segment", None, "vol", None),
            P("segment", None, None, None),
            P("segment", None, None, None),
        ),
        out_specs=(
            P("segment", None, "vol", None),
            P("segment", None, None, None),
            P("segment", None, None, None),
        ),
        check_vma=False,
    )
```

```python
import functools
import math

import jax
import jax.numpy as jnp
from jax import lax
from jax.experimental import pallas as pl
from jax.experimental.pallas import tpu as pltpu
from jax.sharding import PartitionSpec as P

XL = 16
HX = XL // 2
TAPS = 27
BF = jnp.bfloat16
F32 = jnp.float32


def iota(shape, dim):
    return lax.broadcasted_iota(jnp.int32, shape, dim)


def matmul(a, b):
    return lax.dot_general(a, b, (((1,), (0,)), ((), ())), preferred_element_type=F32)


def matmul_nt(a, b):
    return lax.dot_general(a, b, (((1,), (1,)), ((), ())), preferred_element_type=F32)


def tap_mask(lanes, plane, columns, row_step, col_step):
    lane = iota((1, lanes), 1)
    column = lax.rem(lane, columns) - col_step
    row = lax.div(lax.rem(lane, plane), columns) - row_step
    rows = plane // columns
    inside = (column >= 0) & (column < columns) & (row >= 0) & (row < rows)
    return jnp.where(inside, 1.0, 0.0).astype(BF)


def rolled(value, shift):
    size = value.shape[1]
    shift = shift % size
    return value if shift == 0 else pltpu.roll(value, shift, 1)


def kernel(
    sizes,
    class_weight, cotangent, labels, saved, fine_pre, coarse_pre, pooled, fine_w, coarse_w,
    out, collected,
    seed, fine_cat, coarse_cat, pre_rows, pool_rows, pre_ext, grad_ext, pool_ext, pool_out,
    coarse_gate, fine_x, coarse_x, fine_cols, coarse_cols, parts, arrived,
    row_send, row_recv, halo_send, halo_recv, step_send, step_recv, sum_send, sum_recv,
    all_send, all_recv,
):
    segments, n, channels, depth, plane, per, chunks = sizes
    cw = plane // 4
    cdepth = depth // 2
    own = depth * plane
    row_len = coarse_pre.shape[1]
    s = lax.axis_index("segment")
    v = lax.axis_index("vol")
    has_left, has_right = v > 0, v < n - 1
    last = s == segments - 1

    def put(src, dst, send, recv, segment, vol):
        return pltpu.make_async_remote_copy(
            src_ref=src, dst_ref=dst, send_sem=send, recv_sem=recv,
            device_id=(segment, vol), device_id_type=pl.DeviceIdType.MESH,
        )

    barrier = pltpu.get_barrier_semaphore()

    def greet(off, carry):
        pl.semaphore_signal(
            barrier, inc=1, device_id=(s, lax.rem(v + off, n)),
            device_id_type=pl.DeviceIdType.MESH,
        )
        return carry

    lax.fori_loop(1, n, greet, 0)
    for up in (-1, 1):
        for side in (-1, 0, 1):
            there = (s + up >= 0) & (s + up < segments) & (v + side >= 0) & (v + side < n)

            @pl.when(there)
            def _(up=up, side=side):
                pl.semaphore_signal(
                    barrier, inc=1, device_id=(s + up, v + side),
                    device_id_type=pl.DeviceIdType.MESH,
                )

    ups = jnp.where(s > 0, 1, 0) + jnp.where(last, 0, 1)
    sides = 1 + jnp.where(has_left, 1, 0) + jnp.where(has_right, 1, 0)
    pl.semaphore_wait(barrier, n - 1 + ups * sides)

    to_left = put(
        fine_pre.at[0], pre_ext.at[depth + 1],
        halo_send.at[0], halo_recv.at[0], s, v - 1,
    )
    to_right = put(
        fine_pre.at[depth - 1], pre_ext.at[0],
        halo_send.at[1], halo_recv.at[1], s, v + 1,
    )

    def row_copy(which, off):
        src, dst = ((coarse_pre, pre_rows), (pooled, pool_rows))[which]
        return put(
            src, dst.at[v], row_send.at[which, off], row_recv.at[which, v],
            s, lax.rem(v + off, n),
        )

    def send_rows(which):
        def body(off, carry):
            row_copy(which, off).start()
            return carry

        lax.fori_loop(1, n, body, 0)

    def wait_rows(which):
        src, dst = ((coarse_pre, pre_rows), (pooled, pool_rows))[which]

        def body(off, carry):
            u = lax.rem(v + off, n)
            put(src, dst.at[u], row_send.at[which, off], row_recv.at[which, u], s, u).wait_recv()
            return carry

        lax.fori_loop(1, n, body, 0)

    fine_lane = iota((1, own), 1)
    pool_target = (
        lax.div(fine_lane, 2 * plane) * cw
        + lax.div(lax.rem(fine_lane, plane), 2 * XL) * HX
        + lax.div(lax.rem(fine_lane, XL), 2)
    )
    pool_matrix = jnp.where(iota((cdepth * cw, own), 0) == pool_target, 1.0, 0.0).astype(BF)

    def step_copies(src, turn, segment):
        def step(which, a, b, vol):
            return put(a, b, step_send.at[turn, which], step_recv.at[which], segment, vol)

        block = pool_out.at[turn]
        return (
            step(0, src, grad_ext.at[1:depth + 1], v),
            step(1, src.at[0], grad_ext.at[depth + 1], v - 1),
            step(2, src.at[depth - 1], grad_ext.at[0], v + 1),
            step(3, block, pool_ext.at[1], v),
            step(4, block, pool_ext.at[2], v - 1),
            step(5, block, pool_ext.at[0], v + 1),
        )

    def guarded(copies, act, with_own):
        @pl.when(has_left)
        def _():
            act(copies[4])

        @pl.when(has_right)
        def _():
            act(copies[5])

        if with_own:
            act(copies[3])

        @pl.when(has_left)
        def _():
            act(copies[1])

        @pl.when(has_right)
        def _():
            act(copies[2])

        if with_own:
            act(copies[0])

    def joined(ref):
        return jnp.concatenate([ref[p] for p in range(depth)], axis=1)

    send_rows(0)

    @pl.when(last)
    def _():
        for p in range(depth):
            label = labels[p:p + 1, :]
            weight = jnp.zeros(label.shape, F32)
            for index in range(class_weight.shape[0]):
                weight = weight + jnp.where(label == index, class_weight[index], 0.0)
            block = (cotangent[p].astype(F32) * weight).astype(BF)
            seed[p] = block
            grad_ext[p + 1] = block
        pool_out[0] = matmul_nt(joined(seed), pool_matrix).astype(BF)
        guarded(step_copies(seed, 0, s), lambda c: c.start(), False)
        pool_ext[1] = pool_out[0]

    @pl.when(has_left)
    def _():
        to_left.start()

    @pl.when(has_right)
    def _():
        to_right.start()

    for k in range(TAPS):
        rows = slice(k // 9 * channels, (k // 9 + 1) * channels)
        lanes = slice(k % 9 * channels, (k % 9 + 1) * channels)
        coarse_cat[rows, lanes] = coarse_w[k]
        fine_cat[rows, lanes] = fine_w[k]
    for outer in range(3):
        rows = slice(outer * channels, (outer + 1) * channels)
        for p in range(depth + 2):
            q = p - 2 + outer
            block = saved[q] if 0 <= q < depth else jnp.zeros((channels, plane), BF)
            fine_x[rows, p * plane:(p + 1) * plane] = block
    for p in range(depth):
        pre_ext[p + 1] = fine_pre[p]
    pre_rows[v] = coarse_pre[...]
    pool_rows[v] = pooled[...]

    @pl.when(v == 0)
    def _():
        pre_ext[0] = jnp.zeros((channels, plane), BF)
        grad_ext[0] = jnp.zeros((channels, plane), BF)
        pool_ext[0] = jnp.zeros(pool_ext.shape[1:], BF)

    @pl.when(v == n - 1)
    def _():
        pre_ext[depth + 1] = jnp.zeros((channels, plane), BF)
        grad_ext[depth + 1] = jnp.zeros((channels, plane), BF)
        pool_ext[2] = jnp.zeros(pool_ext.shape[1:], BF)

    up_lane = iota((1, plane), 1)
    up_target = lax.div(up_lane, 2 * XL) * HX + lax.div(lax.rem(up_lane, XL), 2)
    up_matrix = jnp.where(iota((cw, plane), 0) == up_target, 0.125, 0.0).astype(BF)

    def gathered(rows, first, planes, low, high):
        lane = iota((1, planes * cw), 1)
        slab = lax.div(lane, cw)
        target = (first + slab) * HX + lax.rem(lane, HX)
        target = jnp.where((slab >= low) & (slab < high), target, -1)
        inline = lax.div(lax.rem(lane, cw), HX)
        row = iota((row_len, planes * cw), 0)

        def body(u, total):
            pick = jnp.where(row == jnp.where(inline == u, target, -1), 1.0, 0.0).astype(BF)
            return total + matmul(rows[u], pick)

        return lax.fori_loop(0, n, body, jnp.zeros((channels, planes * cw), F32))

    wait_rows(0)
    send_rows(1)
    reach = cdepth + 4
    coarse_gate[...] = gathered(pre_rows, v * cdepth - 2, reach, 0, reach).astype(BF)

    def take_pooled():
        wait_rows(1)
        own_x = gathered(pool_rows, v * cdepth - 2, reach, 2, 2 + cdepth).astype(BF)
        for outer in range(3):
            coarse_x[outer * channels:(outer + 1) * channels, :] = rolled(own_x, (1 - outer) * cw)

    @pl.when(jnp.logical_not(last))
    def _():
        take_pooled()

    incoming = step_copies(out, 1, s)

    def wait_incoming(middle, left, right):
        @pl.when(jnp.logical_not(last))
        def _():
            incoming[middle].wait_recv()

        @pl.when(has_left)
        def _():
            incoming[left].wait_recv()

        @pl.when(has_right)
        def _():
            incoming[right].wait_recv()

    wait_incoming(3, 5, 4)

    def place(which, k, value):
        at = (k % per) * channels
        parts[which, k // per, :, at:at + channels] = value

    def chunk_of(which, vol):
        return vol if which == 0 else n - 1 - vol

    def sum_copy(which, off, vol_from, vol_to, chunk):
        return put(
            parts.at[which, chunk], arrived.at[which, vol_from],
            sum_send.at[which, off], sum_recv.at[which, vol_from], s, vol_to,
        )

    def start_sums(which):
        for k in range(TAPS, chunks * per):
            place(which, k, jnp.zeros((channels, channels), BF))

        def body(off, carry):
            t = lax.rem(v + off, n)
            chunk = chunk_of(which, t)

            @pl.when(chunk < chunks)
            def _():
                sum_copy(which, off, v, t, chunk).start()

            return carry

        lax.fori_loop(1, n, body, 0)

    def place_all(which, grads):
        for k in range(TAPS):
            rows = slice(k // 9 * channels, (k // 9 + 1) * channels)
            place(which, k, grads[rows, k % 9 * channels:(k % 9 + 1) * channels])
        start_sums(which)

    def fine_sums():
        place_all(0, matmul_nt(fine_x[...], fine_cols[...]).astype(BF))

    def coarse_sums():
        place_all(1, matmul_nt(coarse_x[...], coarse_cols[...]).astype(BF))

    side = pool_ext.shape[2]
    near = jnp.concatenate(
        [pool_ext[0][:, side - 2 * cw:], pool_ext[1], pool_ext[2][:, :2 * cw]], axis=1
    )
    coarse_gz = jnp.where(coarse_gate[...] > 0, near, jnp.zeros_like(near))
    for row_step in (-1, 0, 1):
        for col_step in (-1, 0, 1):
            mask = tap_mask(reach * cw, cw, HX, row_step, col_step)
            r = (row_step + 1) * 3 + col_step + 1
            coarse_cols[r * channels:(r + 1) * channels, :] = (
                rolled(coarse_gz, row_step * HX + col_step) * mask
            )

    @pl.when(s == 0)
    def _():
        coarse_sums()

    def over_depth(terms, step, width):
        return sum(
            terms[outer * channels:(outer + 1) * channels, (2 - outer) * step:(2 - outer) * step + width]
            for outer in range(3)
        )

    terms = matmul(coarse_cat[...], coarse_cols[...])
    coarse_back = over_depth(terms, cw, (cdepth + 2) * cw).astype(BF)

    pieces = []
    for p in range(depth + 2):
        j = (p + 1) // 2
        if p and j == p // 2:
            spread = pieces[-1]
        else:
            spread = matmul(coarse_back[:, j * cw:(j + 1) * cw], up_matrix)
        pieces.append(spread)

    @pl.when(has_left)
    def _():
        to_right.wait_recv()

    @pl.when(has_right)
    def _():
        to_left.wait_recv()

    wait_incoming(0, 2, 1)
    gz = []
    for p in range(depth + 2):
        grad = grad_ext[p].astype(F32) + pieces[p]
        gz.append(jnp.where(pre_ext[p].astype(F32) > 0, grad, 0.0).astype(BF))
    for row_step in (-1, 0, 1):
        for col_step in (-1, 0, 1):
            mask = tap_mask(plane, plane, XL, row_step, col_step)
            r = (row_step + 1) * 3 + col_step + 1
            for p in range(depth + 2):
                fine_cols[r * channels:(r + 1) * channels, p * plane:(p + 1) * plane] = (
                    rolled(gz[p], row_step * XL + col_step) * mask
                )
    @pl.when(s == 0)
    def _():
        fine_sums()

    total = over_depth(matmul(fine_cat[...], fine_cols[...]), plane, own)
    total = total + jnp.concatenate([grad_ext[p + 1].astype(F32) for p in range(depth)], axis=1)
    for p in range(depth):
        out[p] = total[:, p * plane:(p + 1) * plane].astype(BF)

    @pl.when(s > 0)
    def _():
        pool_out[1] = matmul_nt(joined(out), pool_matrix).astype(BF)
        guarded(step_copies(out, 1, s - 1), lambda c: c.start(), True)

    @pl.when(s > 0)
    def _():
        fine_sums()

        @pl.when(last)
        def _():
            take_pooled()

        coarse_sums()

    def all_copy(which, off, chunk, vol_to):
        return put(
            collected.at[which, chunk], collected.at[which, chunk],
            all_send.at[which, off], all_recv.at[which, chunk], s, vol_to,
        )

    for which in (1, 0):
        mine = chunk_of(which, v)

        @pl.when(mine < chunks)
        def _(which=which, mine=mine):
            def add(off, carry):
                u = lax.rem(v + off, n)
                sum_copy(which, off, u, u, mine).wait_recv()
                return carry + arrived[which, u].astype(F32)

            whole = lax.fori_loop(1, n, add, parts[which, mine].astype(F32))
            collected[which, mine] = whole.astype(BF)

            def hand(off, carry):
                all_copy(which, off, mine, lax.rem(v + off, n)).start()
                return carry

            lax.fori_loop(1, n, hand, 0)

    for which in (0, 1):
        mine = chunk_of(which, v)

        def rest(off, carry, which=which, mine=mine):
            t = lax.rem(v + off, n)
            row_copy(which, off).wait_send()
            chunk = chunk_of(which, t)

            @pl.when(chunk < chunks)
            def _():
                sum_copy(which, off, v, t, chunk).wait_send()
                all_copy(which, off, chunk, t).wait_recv()

            @pl.when(mine < chunks)
            def _():
                all_copy(which, off, mine, t).wait_send()

            return carry

        lax.fori_loop(1, n, rest, 0)

    @pl.when(has_left)
    def _():
        to_left.wait_send()

    @pl.when(has_right)
    def _():
        to_right.wait_send()

    @pl.when(last)
    def _():
        guarded(step_copies(seed, 0, s), lambda c: c.wait_send(), False)

    @pl.when(s > 0)
    def _():
        guarded(step_copies(out, 1, s - 1), lambda c: c.wait_send(), True)


def finish(per, scales, collected, fine_out, coarse_out):
    channels = fine_out.shape[1]
    for which, ref in enumerate((fine_out, coarse_out)):
        for k in range(TAPS):
            at = (k % per) * channels
            value = collected[which, k // per, :, at:at + channels]
            ref[k] = value.astype(F32) * scales[which]


def on_device(
    cotangent, labels, class_weight, inputs, fine_pre, pooled, coarse_pre,
    fine_filters, coarse_filters,
):
    segments = lax.axis_size("segment")
    n = lax.axis_size("vol")
    channels, depth, plane = inputs.shape[1:]
    own = depth * plane
    cw = plane // 4
    cdepth = depth // 2
    row_len = pooled.shape[2] * pooled.shape[3]
    per = -(-TAPS // n)
    chunks = -(-TAPS // per)
    cells = own * n
    scales = (1.0 / math.sqrt(cells), 1.0 / math.sqrt(cells // 8))
    sizes = (segments, n, channels, depth, plane, per, chunks)
    chunk_shape = (channels, per * channels)
    vmem = pl.BlockSpec(memory_space=pltpu.VMEM)
    dma = pltpu.SemaphoreType.DMA
    grad, collected = pl.pallas_call(
        functools.partial(kernel, sizes),
        out_shape=(
            jax.ShapeDtypeStruct((depth, channels, plane), BF),
            jax.ShapeDtypeStruct((2, chunks, *chunk_shape), BF),
        ),
        in_specs=[pl.BlockSpec(memory_space=pltpu.SMEM)] + [vmem] * 8,
        out_specs=(vmem, vmem),
        scratch_shapes=[
            pltpu.VMEM((depth, channels, plane), BF),
            pltpu.VMEM((3 * channels, 9 * channels), BF),
            pltpu.VMEM((3 * channels, 9 * channels), BF),
            pltpu.VMEM((n, channels, row_len), BF),
            pltpu.VMEM((n, channels, row_len), BF),
            pltpu.VMEM((depth + 2, channels, plane), BF),
            pltpu.VMEM((depth + 2, channels, plane), BF),
            pltpu.VMEM((3, channels, cdepth * cw), BF),
            pltpu.VMEM((2, channels, cdepth * cw), BF),
            pltpu.VMEM((channels, (cdepth + 4) * cw), BF),
            pltpu.VMEM((3 * channels, own + 2 * plane), BF),
            pltpu.VMEM((3 * channels, (cdepth + 4) * cw), BF),
            pltpu.VMEM((9 * channels, own + 2 * plane), BF),
            pltpu.VMEM((9 * channels, (cdepth + 4) * cw), BF),
            pltpu.VMEM((2, chunks, *chunk_shape), BF),
            pltpu.VMEM((2, n, *chunk_shape), BF),
            dma((2, n)), dma((2, n)), dma((2,)), dma((2,)), dma((2, 6)), dma((6,)),
            dma((2, n)), dma((2, n)), dma((2, n)), dma((2, chunks)),
        ],
        compiler_params=pltpu.CompilerParams(
            collective_id=0, has_side_effects=True, vmem_limit_bytes=60 * 1024 * 1024
        ),
    )(
        class_weight,
        cotangent.transpose(1, 0, 2),
        labels,
        inputs[0].transpose(1, 0, 2),
        fine_pre[0].transpose(1, 0, 2),
        coarse_pre[0].reshape(channels, row_len),
        pooled[0].reshape(channels, row_len),
        fine_filters[0],
        coarse_filters[0],
    )

    tap_shape = jax.ShapeDtypeStruct((TAPS, channels, channels), F32)
    fine_grads, coarse_grads = pl.pallas_call(
        functools.partial(finish, per, scales),
        out_shape=(tap_shape, tap_shape),
        in_specs=[vmem],
        out_specs=(vmem, vmem),
    )(collected)
    return (grad.transpose(1, 0, 2)[None], fine_grads[None], coarse_grads[None])


def solution(mesh):
    return jax.shard_map(
        on_device,
        mesh=mesh,
        in_specs=(
            P(None, "vol", None),
            P("vol", None),
            P(),
            P("segment", None, "vol", None),
            P("segment", None, "vol", None),
            P("segment", None, "vol", None),
            P("segment", None, "vol", None),
            P("segment", None, None, None),
            P("segment", None, None, None),
        ),
        out_specs=(
            P("segment", None, "vol", None),
            P("segment", None, None, None),
            P("segment", None, None, None),
        ),
        check_vma=False,
    )
```

```python
import functools
import math

import jax
import jax.numpy as jnp
from jax import lax
from jax.experimental import pallas as pl
from jax.experimental.pallas import tpu as pltpu
from jax.sharding import PartitionSpec as P

XL = 16
HX = XL // 2
TAPS = 27
BF = jnp.bfloat16
F32 = jnp.float32


def iota(shape, dim):
    return lax.broadcasted_iota(jnp.int32, shape, dim)


def matmul(a, b):
    return lax.dot_general(a, b, (((1,), (0,)), ((), ())), preferred_element_type=F32)


def matmul_nt(a, b):
    return lax.dot_general(a, b, (((1,), (1,)), ((), ())), preferred_element_type=F32)


def tap_mask(lanes, plane, columns, row_step, col_step):
    lane = iota((1, lanes), 1)
    column = lax.rem(lane, columns) - col_step
    row = lax.div(lax.rem(lane, plane), columns) - row_step
    rows = plane // columns
    inside = (column >= 0) & (column < columns) & (row >= 0) & (row < rows)
    return jnp.where(inside, 1.0, 0.0).astype(BF)


def rolled(value, shift):
    size = value.shape[1]
    shift = shift % size
    return value if shift == 0 else pltpu.roll(value, shift, 1)


def kernel(
    sizes,
    class_weight, cotangent, labels, saved, fine_pre, coarse_pre, pooled, fine_w, coarse_w,
    out, collected,
    seed, fine_cat, coarse_cat, pre_rows, pool_rows, pre_ext, grad_ext, pool_ext, pool_out,
    coarse_gate, fine_x, coarse_x, fine_cols, coarse_cols, parts, arrived,
    row_send, row_recv, halo_send, halo_recv, step_send, step_recv, sum_send, sum_recv,
    all_send, all_recv,
):
    segments, n, channels, depth, plane, per, chunks = sizes
    cw = plane // 4
    cdepth = depth // 2
    own = depth * plane
    row_len = coarse_pre.shape[1]
    s = lax.axis_index("segment")
    v = lax.axis_index("vol")
    has_left, has_right = v > 0, v < n - 1
    last = s == segments - 1

    def put(src, dst, send, recv, segment, vol):
        return pltpu.make_async_remote_copy(
            src_ref=src, dst_ref=dst, send_sem=send, recv_sem=recv,
            device_id=(segment, vol), device_id_type=pl.DeviceIdType.MESH,
        )

    barrier = pltpu.get_barrier_semaphore()

    def greet(off, carry):
        pl.semaphore_signal(
            barrier, inc=1, device_id=(s, lax.rem(v + off, n)),
            device_id_type=pl.DeviceIdType.MESH,
        )
        return carry

    lax.fori_loop(1, n, greet, 0)
    for up in (-1, 1):
        for side in (-1, 0, 1):
            there = (s + up >= 0) & (s + up < segments) & (v + side >= 0) & (v + side < n)

            @pl.when(there)
            def _(up=up, side=side):
                pl.semaphore_signal(
                    barrier, inc=1, device_id=(s + up, v + side),
                    device_id_type=pl.DeviceIdType.MESH,
                )

    ups = jnp.where(s > 0, 1, 0) + jnp.where(last, 0, 1)
    sides = 1 + jnp.where(has_left, 1, 0) + jnp.where(has_right, 1, 0)
    pl.semaphore_wait(barrier, n - 1 + ups * sides)

    to_left = put(
        pre_ext.at[1], pre_ext.at[depth + 1],
        halo_send.at[0], halo_recv.at[0], s, v - 1,
    )
    to_right = put(
        pre_ext.at[depth], pre_ext.at[0],
        halo_send.at[1], halo_recv.at[1], s, v + 1,
    )

    def row_copy(which, off):
        src, dst = ((coarse_pre, pre_rows), (pooled, pool_rows))[which]
        return put(
            src, dst.at[v], row_send.at[which, off], row_recv.at[which, v],
            s, lax.rem(v + off, n),
        )

    def send_rows(which):
        def body(off, carry):
            row_copy(which, off).start()
            return carry

        lax.fori_loop(1, n, body, 0)

    def wait_rows(which):
        src, dst = ((coarse_pre, pre_rows), (pooled, pool_rows))[which]

        def body(off, carry):
            u = lax.rem(v + off, n)
            put(src, dst.at[u], row_send.at[which, off], row_recv.at[which, u], s, u).wait_recv()
            return carry

        lax.fori_loop(1, n, body, 0)

    fine_lane = iota((1, own), 1)
    pool_target = (
        lax.div(fine_lane, 2 * plane) * cw
        + lax.div(lax.rem(fine_lane, plane), 2 * XL) * HX
        + lax.div(lax.rem(fine_lane, XL), 2)
    )
    pool_matrix = jnp.where(iota((cdepth * cw, own), 0) == pool_target, 1.0, 0.0).astype(BF)

    def step_copies(src, turn, segment):
        def step(which, a, b, vol):
            return put(a, b, step_send.at[turn, which], step_recv.at[which], segment, vol)

        block = pool_out.at[turn]
        return (
            step(0, src, grad_ext.at[1:depth + 1], v),
            step(1, src.at[0], grad_ext.at[depth + 1], v - 1),
            step(2, src.at[depth - 1], grad_ext.at[0], v + 1),
            step(3, block, pool_ext.at[1], v),
            step(4, block, pool_ext.at[2], v - 1),
            step(5, block, pool_ext.at[0], v + 1),
        )

    def guarded(copies, act, with_own):
        @pl.when(has_left)
        def _():
            act(copies[4])

        @pl.when(has_right)
        def _():
            act(copies[5])

        if with_own:
            act(copies[3])

        @pl.when(has_left)
        def _():
            act(copies[1])

        @pl.when(has_right)
        def _():
            act(copies[2])

        if with_own:
            act(copies[0])

    def joined(ref):
        return jnp.concatenate([ref[p] for p in range(depth)], axis=1)

    send_rows(0)

    @pl.when(last)
    def _():
        planes = jnp.swapaxes(cotangent[...], 0, 1)
        for p in range(depth):
            label = labels[p:p + 1, :]
            weight = jnp.zeros(label.shape, F32)
            for index in range(class_weight.shape[0]):
                weight = weight + jnp.where(label == index, class_weight[index], 0.0)
            block = (planes[p].astype(F32) * weight).astype(BF)
            seed[p] = block
            grad_ext[p + 1] = block
        pool_out[0] = matmul_nt(joined(seed), pool_matrix).astype(BF)
        guarded(step_copies(seed, 0, s), lambda c: c.start(), False)
        pool_ext[1] = pool_out[0]

    pre_ext[1:depth + 1] = jnp.swapaxes(fine_pre[...], 0, 1)

    @pl.when(has_left)
    def _():
        to_left.start()

    @pl.when(has_right)
    def _():
        to_right.start()

    for k in range(TAPS):
        rows = slice(k // 9 * channels, (k // 9 + 1) * channels)
        lanes = slice(k % 9 * channels, (k % 9 + 1) * channels)
        coarse_cat[rows, lanes] = coarse_w[k]
        fine_cat[rows, lanes] = fine_w[k]
    planes = jnp.swapaxes(saved[...], 0, 1)
    for outer in range(3):
        rows = slice(outer * channels, (outer + 1) * channels)
        for p in range(depth + 2):
            q = p - 2 + outer
            block = planes[q] if 0 <= q < depth else jnp.zeros((channels, plane), BF)
            fine_x[rows, p * plane:(p + 1) * plane] = block
    pre_rows[v] = coarse_pre[...]
    pool_rows[v] = pooled[...]

    @pl.when(v == 0)
    def _():
        pre_ext[0] = jnp.zeros((channels, plane), BF)
        grad_ext[0] = jnp.zeros((channels, plane), BF)
        pool_ext[0] = jnp.zeros(pool_ext.shape[1:], BF)

    @pl.when(v == n - 1)
    def _():
        pre_ext[depth + 1] = jnp.zeros((channels, plane), BF)
        grad_ext[depth + 1] = jnp.zeros((channels, plane), BF)
        pool_ext[2] = jnp.zeros(pool_ext.shape[1:], BF)

    up_lane = iota((1, plane), 1)
    up_target = lax.div(up_lane, 2 * XL) * HX + lax.div(lax.rem(up_lane, XL), 2)
    up_matrix = jnp.where(iota((cw, plane), 0) == up_target, 0.125, 0.0).astype(BF)

    def gathered(rows, first, planes, low, high):
        lane = iota((1, planes * cw), 1)
        slab = lax.div(lane, cw)
        target = (first + slab) * HX + lax.rem(lane, HX)
        target = jnp.where((slab >= low) & (slab < high), target, -1)
        inline = lax.div(lax.rem(lane, cw), HX)
        row = iota((row_len, planes * cw), 0)

        def body(u, total):
            pick = jnp.where(row == jnp.where(inline == u, target, -1), 1.0, 0.0).astype(BF)
            return total + matmul(rows[u], pick)

        return lax.fori_loop(0, n, body, jnp.zeros((channels, planes * cw), F32))

    wait_rows(0)
    send_rows(1)
    reach = cdepth + 4
    coarse_gate[...] = gathered(pre_rows, v * cdepth - 2, reach, 0, reach).astype(BF)

    def take_pooled():
        wait_rows(1)
        own_x = gathered(pool_rows, v * cdepth - 2, reach, 2, 2 + cdepth).astype(BF)
        for outer in range(3):
            coarse_x[outer * channels:(outer + 1) * channels, :] = rolled(own_x, (1 - outer) * cw)

    @pl.when(jnp.logical_not(last))
    def _():
        take_pooled()

    incoming = step_copies(out, 1, s)

    def wait_incoming(middle, left, right):
        @pl.when(jnp.logical_not(last))
        def _():
            incoming[middle].wait_recv()

        @pl.when(has_left)
        def _():
            incoming[left].wait_recv()

        @pl.when(has_right)
        def _():
            incoming[right].wait_recv()

    wait_incoming(3, 5, 4)

    def place(which, k, value):
        at = (k % per) * channels
        parts[which, k // per, :, at:at + channels] = value

    def chunk_of(which, vol):
        return vol if which == 0 else n - 1 - vol

    def sum_copy(which, off, vol_from, vol_to, chunk):
        return put(
            parts.at[which, chunk], arrived.at[which, vol_from],
            sum_send.at[which, off], sum_recv.at[which, vol_from], s, vol_to,
        )

    def start_sums(which):
        for k in range(TAPS, chunks * per):
            place(which, k, jnp.zeros((channels, channels), BF))

        def body(off, carry):
            t = lax.rem(v + off, n)
            chunk = chunk_of(which, t)

            @pl.when(chunk < chunks)
            def _():
                sum_copy(which, off, v, t, chunk).start()

            return carry

        lax.fori_loop(1, n, body, 0)

    def place_all(which, grads):
        for k in range(TAPS):
            rows = slice(k // 9 * channels, (k // 9 + 1) * channels)
            place(which, k, grads[rows, k % 9 * channels:(k % 9 + 1) * channels])
        start_sums(which)

    def fine_sums():
        place_all(0, matmul_nt(fine_x[...], fine_cols[...]).astype(BF))

    def coarse_sums():
        place_all(1, matmul_nt(coarse_x[...], coarse_cols[...]).astype(BF))

    side = pool_ext.shape[2]
    near = jnp.concatenate(
        [pool_ext[0][:, side - 2 * cw:], pool_ext[1], pool_ext[2][:, :2 * cw]], axis=1
    )
    coarse_gz = jnp.where(coarse_gate[...] > 0, near, jnp.zeros_like(near))
    for row_step in (-1, 0, 1):
        for col_step in (-1, 0, 1):
            mask = tap_mask(reach * cw, cw, HX, row_step, col_step)
            r = (row_step + 1) * 3 + col_step + 1
            coarse_cols[r * channels:(r + 1) * channels, :] = (
                rolled(coarse_gz, row_step * HX + col_step) * mask
            )

    @pl.when(s == 0)
    def _():
        coarse_sums()

    def over_depth(terms, step, width):
        return sum(
            terms[outer * channels:(outer + 1) * channels, (2 - outer) * step:(2 - outer) * step + width]
            for outer in range(3)
        )

    terms = matmul(coarse_cat[...], coarse_cols[...])
    coarse_back = over_depth(terms, cw, (cdepth + 2) * cw).astype(BF)

    pieces = []
    for p in range(depth + 2):
        j = (p + 1) // 2
        if p and j == p // 2:
            spread = pieces[-1]
        else:
            spread = matmul(coarse_back[:, j * cw:(j + 1) * cw], up_matrix)
        pieces.append(spread)

    @pl.when(has_left)
    def _():
        to_right.wait_recv()

    @pl.when(has_right)
    def _():
        to_left.wait_recv()

    wait_incoming(0, 2, 1)
    gz = []
    for p in range(depth + 2):
        grad = grad_ext[p].astype(F32) + pieces[p]
        gz.append(jnp.where(pre_ext[p].astype(F32) > 0, grad, 0.0).astype(BF))
    for row_step in (-1, 0, 1):
        for col_step in (-1, 0, 1):
            mask = tap_mask(plane, plane, XL, row_step, col_step)
            r = (row_step + 1) * 3 + col_step + 1
            for p in range(depth + 2):
                fine_cols[r * channels:(r + 1) * channels, p * plane:(p + 1) * plane] = (
                    rolled(gz[p], row_step * XL + col_step) * mask
                )
    @pl.when(s == 0)
    def _():
        fine_sums()

    total = over_depth(matmul(fine_cat[...], fine_cols[...]), plane, own)
    total = total + jnp.concatenate([grad_ext[p + 1].astype(F32) for p in range(depth)], axis=1)
    for p in range(depth):
        out[p] = total[:, p * plane:(p + 1) * plane].astype(BF)

    @pl.when(s > 0)
    def _():
        pool_out[1] = matmul_nt(joined(out), pool_matrix).astype(BF)
        guarded(step_copies(out, 1, s - 1), lambda c: c.start(), True)

    @pl.when(s > 0)
    def _():
        fine_sums()

        @pl.when(last)
        def _():
            take_pooled()

        coarse_sums()

    def all_copy(which, off, chunk, vol_to):
        return put(
            collected.at[which, chunk], collected.at[which, chunk],
            all_send.at[which, off], all_recv.at[which, chunk], s, vol_to,
        )

    for which in (1, 0):
        mine = chunk_of(which, v)

        @pl.when(mine < chunks)
        def _(which=which, mine=mine):
            def add(off, carry):
                u = lax.rem(v + off, n)
                sum_copy(which, off, u, u, mine).wait_recv()
                return carry + arrived[which, u].astype(F32)

            whole = lax.fori_loop(1, n, add, parts[which, mine].astype(F32))
            collected[which, mine] = whole.astype(BF)

            def hand(off, carry):
                all_copy(which, off, mine, lax.rem(v + off, n)).start()
                return carry

            lax.fori_loop(1, n, hand, 0)

    for which in (0, 1):
        mine = chunk_of(which, v)

        def rest(off, carry, which=which, mine=mine):
            t = lax.rem(v + off, n)
            row_copy(which, off).wait_send()
            chunk = chunk_of(which, t)

            @pl.when(chunk < chunks)
            def _():
                sum_copy(which, off, v, t, chunk).wait_send()
                all_copy(which, off, chunk, t).wait_recv()

            @pl.when(mine < chunks)
            def _():
                all_copy(which, off, mine, t).wait_send()

            return carry

        lax.fori_loop(1, n, rest, 0)

    @pl.when(has_left)
    def _():
        to_left.wait_send()

    @pl.when(has_right)
    def _():
        to_right.wait_send()

    @pl.when(last)
    def _():
        guarded(step_copies(seed, 0, s), lambda c: c.wait_send(), False)

    @pl.when(s > 0)
    def _():
        guarded(step_copies(out, 1, s - 1), lambda c: c.wait_send(), True)


def finish(per, scales, grad, collected, grad_out, fine_out, coarse_out):
    channels = fine_out.shape[1]
    grad_out[...] = jnp.swapaxes(grad[...], 0, 1)
    for which, ref in enumerate((fine_out, coarse_out)):
        for k in range(TAPS):
            at = (k % per) * channels
            value = collected[which, k // per, :, at:at + channels]
            ref[k] = value.astype(F32) * scales[which]


def on_device(
    cotangent, labels, class_weight, inputs, fine_pre, pooled, coarse_pre,
    fine_filters, coarse_filters,
):
    segments = lax.axis_size("segment")
    n = lax.axis_size("vol")
    channels, depth, plane = inputs.shape[1:]
    own = depth * plane
    cw = plane // 4
    cdepth = depth // 2
    row_len = pooled.shape[2] * pooled.shape[3]
    per = -(-TAPS // n)
    chunks = -(-TAPS // per)
    cells = own * n
    scales = (1.0 / math.sqrt(cells), 1.0 / math.sqrt(cells // 8))
    sizes = (segments, n, channels, depth, plane, per, chunks)
    chunk_shape = (channels, per * channels)
    vmem = pl.BlockSpec(memory_space=pltpu.VMEM)
    dma = pltpu.SemaphoreType.DMA
    grad, collected = pl.pallas_call(
        functools.partial(kernel, sizes),
        out_shape=(
            jax.ShapeDtypeStruct((depth, channels, plane), BF),
            jax.ShapeDtypeStruct((2, chunks, *chunk_shape), BF),
        ),
        in_specs=[pl.BlockSpec(memory_space=pltpu.SMEM)] + [vmem] * 8,
        out_specs=(vmem, vmem),
        scratch_shapes=[
            pltpu.VMEM((depth, channels, plane), BF),
            pltpu.VMEM((3 * channels, 9 * channels), BF),
            pltpu.VMEM((3 * channels, 9 * channels), BF),
            pltpu.VMEM((n, channels, row_len), BF),
            pltpu.VMEM((n, channels, row_len), BF),
            pltpu.VMEM((depth + 2, channels, plane), BF),
            pltpu.VMEM((depth + 2, channels, plane), BF),
            pltpu.VMEM((3, channels, cdepth * cw), BF),
            pltpu.VMEM((2, channels, cdepth * cw), BF),
            pltpu.VMEM((channels, (cdepth + 4) * cw), BF),
            pltpu.VMEM((3 * channels, own + 2 * plane), BF),
            pltpu.VMEM((3 * channels, (cdepth + 4) * cw), BF),
            pltpu.VMEM((9 * channels, own + 2 * plane), BF),
            pltpu.VMEM((9 * channels, (cdepth + 4) * cw), BF),
            pltpu.VMEM((2, chunks, *chunk_shape), BF),
            pltpu.VMEM((2, n, *chunk_shape), BF),
            dma((2, n)), dma((2, n)), dma((2,)), dma((2,)), dma((2, 6)), dma((6,)),
            dma((2, n)), dma((2, n)), dma((2, n)), dma((2, chunks)),
        ],
        compiler_params=pltpu.CompilerParams(
            collective_id=0, has_side_effects=True, vmem_limit_bytes=60 * 1024 * 1024
        ),
    )(
        class_weight,
        cotangent,
        labels,
        inputs[0],
        fine_pre[0],
        coarse_pre[0].reshape(channels, row_len),
        pooled[0].reshape(channels, row_len),
        fine_filters[0],
        coarse_filters[0],
    )

    tap_shape = jax.ShapeDtypeStruct((TAPS, channels, channels), F32)
    grad, fine_grads, coarse_grads = pl.pallas_call(
        functools.partial(finish, per, scales),
        out_shape=(jax.ShapeDtypeStruct((channels, depth, plane), BF), tap_shape, tap_shape),
        in_specs=[vmem] * 2,
        out_specs=(vmem, vmem, vmem),
    )(grad, collected)
    return (grad[None], fine_grads[None], coarse_grads[None])


def solution(mesh):
    return jax.shard_map(
        on_device,
        mesh=mesh,
        in_specs=(
            P(None, "vol", None),
            P("vol", None),
            P(),
            P("segment", None, "vol", None),
            P("segment", None, "vol", None),
            P("segment", None, "vol", None),
            P("segment", None, "vol", None),
            P("segment", None, None, None),
            P("segment", None, None, None),
        ),
        out_specs=(
            P("segment", None, "vol", None),
            P("segment", None, None, None),
            P("segment", None, None, None),
        ),
        check_vma=False,
    )
```
